256 devices in a mesh: tile: 64 (over z_hi, x, y, core), lev: 4 (over z_lo).
Axes of the slice: x: 4, y: 4, z: 8 (z_hi: 2, z_lo: 4; z = z_hi * 4 + z_lo), core: 2. Of those that a mesh axis runs over, the one named last changes fastest.
Arguments:
- tracers: float32 [64, 8, 8, 72, 128], P('tile', None, None, 'lev'), may hold values from -6 to 6
- courant_first: float32 [64, 8, 8, 72], P('tile', None, None, 'lev'), may hold values from -0.9 to 0.9
- courant_second: float32 [64, 8, 8, 72], P('tile', None, None, 'lev'), may hold values from -0.9 to 0.9
- weights: float32 [64, 8, 8, 72, 72], P('tile', 'lev'), may hold values from 0.05 to 1
- frame_flip: int32 [64, 2], P('tile'), may hold values from 0 to 1
Outputs:
- transported: float32 [64, 8, 8, 72, 128], P('tile', None, None, 'lev')
The draws below stay inside these ranges and needn't reach their ends.
All inputs are finite; a program needn't handle non-finite values.
Results may differ from the reference program's by a relative error of at most 0.0003.
Values sent between devices are 32-bit elements; how exact they have to be, the bound alone decides.
A program may use at most 64 MiB of HBM per device.

```python
import jax
import jax.numpy as jnp
from jax import lax

SIDE = 8
LEVELS = 72
TRACERS = 128
SUBSTEPS = 3
TILES = 64
STRIDE = 8


def set_ends(result, rng, least, high):
    index_at = [jax.random.randint(jax.random.fold_in(rng, axis), (), 0, length) for axis, length in enumerate(result.shape)]
    widest = result.shape.index(max(result.shape))
    beside = index_at[:widest] + [(index_at[widest] + 1) % result.shape[widest]] + index_at[widest + 1:]
    return result.at[tuple(index_at)].set(least).at[tuple(beside)].set(high)


def block_levels(own_key, dims, split, low, high):
    def one(dim, shards_of):
        heights = jax.random.uniform(jax.random.fold_in(jax.random.fold_in(own_key, 6), dim), (shards_of,), jnp.float32, low / len(split), high / len(split))
        return jnp.repeat(jnp.exp(heights), dims[dim] // shards_of).reshape((-1,) + (1,) * (len(dims) - dim - 1))

    gain = one(*split[0])
    for cut in split[1:]:
        gain = gain * one(*cut)
    return gain


def gaussian(stream_key, extent, spread, reach, cuts=(), kind=jnp.bfloat16):
    level = block_levels(stream_key, extent, cuts, -0.22, 0.18) if cuts else 1.0
    array = jax.random.normal(stream_key, extent, jnp.float32) * spread * level
    return jnp.minimum(jnp.maximum(array, -reach), reach).astype(kind)


def setup_inputs(seed: int = 0) -> dict:
    key_of = jax.random.split(jax.random.key(seed), 6)
    return {
        "tracers": gaussian(key_of[0], (TILES, SIDE, SIDE, LEVELS, TRACERS), 1.0, 6.0, ((0, 64), (3, 4)), jnp.float32),
        "courant_first": jnp.clip(jax.random.uniform(key_of[1], (TILES, SIDE, SIDE, LEVELS), jnp.float32, -0.9, 0.9) * block_levels(key_of[1], (TILES, SIDE, SIDE, LEVELS), ((0, 64), (3, 4)), -0.4, 0.0), -0.9, 0.9),
        "courant_second": jnp.clip(jax.random.uniform(key_of[2], (TILES, SIDE, SIDE, LEVELS), jnp.float32, -0.9, 0.9) * block_levels(key_of[2], (TILES, SIDE, SIDE, LEVELS), ((0, 64), (3, 4)), -0.4, 0.0), -0.9, 0.9),
        "weights": jnp.clip(0.05 + 0.95 * jax.random.uniform(key_of[3], (TILES, SIDE, SIDE, LEVELS, LEVELS), jnp.float32) ** block_levels(key_of[3], (TILES, SIDE, SIDE, LEVELS, LEVELS), ((0, 64), (1, 4)), -0.2, 0.2), 0.05, 1.0),
        "frame_flip": set_ends(jax.random.randint(key_of[4], (TILES, 2), 0, 2), jax.random.fold_in(key_of[4], 1), 0, 1).astype(jnp.int32),
    }


group_width = 16


def ppm_update(extended, courant, along):
    length = extended.shape[along] - 6

    def window(values, offset, amount):
        return lax.slice_in_dim(values, offset, offset + amount, axis=along)

    interfaces = (7.0 * (window(extended, 1, length + 3) + window(extended, 2, length + 3)) - (window(extended, 0, length + 3) + window(extended, 3, length + 3))) / 12.0
    low_edge = window(interfaces, 0, length + 2)
    high_edge = window(interfaces, 1, length + 2)
    centre = window(extended, 2, length + 2)
    gradient = high_edge - low_edge
    curvature = 6.0 * centre - 3.0 * (low_edge + high_edge)
    upward = courant * (window(high_edge, 0, length + 1) - 0.5 * courant * (window(gradient, 0, length + 1) - (1.0 - courant * (2.0 / 3.0)) * window(curvature, 0, length + 1)))
    downward = courant * (window(low_edge, 1, length + 1) - 0.5 * courant * (window(gradient, 1, length + 1) + (1.0 + courant * (2.0 / 3.0)) * window(curvature, 1, length + 1)))
    fluxes = jnp.where(courant >= 0.0, upward, downward)
    return window(centre, 1, length) - (window(fluxes, 1, length) - window(fluxes, 0, length))


def to_frame(blocks, flip_flags):
    first_flag = (flip_flags[:, 0] == 1)[:, None, None, None, None]
    second_flag = (flip_flags[:, 1] == 1)[:, None, None, None, None]
    turned = jnp.where(first_flag, blocks[:, ::-1], blocks)
    return jnp.where(second_flag, turned[:, :, ::-1], turned)


def mixing_matrix(weights):
    totals = jnp.sum(weights, axis=-1, keepdims=True)
    identity = jnp.eye(weights.shape[-1], dtype=jnp.float32)
    return 0.6 * identity + 0.4 * (weights / totals)


def reference(tracers, courant_first, courant_second, weights, frame_flip):
    mixing = mixing_matrix(weights)
    first_faces = jnp.concatenate([jnp.roll(courant_first, STRIDE, axis=0)[:, SIDE - 1:], courant_first], axis=1)[..., None]
    second_faces = jnp.concatenate([jnp.roll(courant_second, 1, axis=0)[:, :, SIDE - 1:], courant_second], axis=2)[..., None]

    def advance(blocks):
        fields = to_frame(blocks, frame_flip)
        for substep in range(SUBSTEPS):
            extended = jnp.concatenate([jnp.roll(fields, STRIDE, axis=0)[:, SIDE - 3:], fields, jnp.roll(fields, -STRIDE, axis=0)[:, :3]], axis=1)
            fields = ppm_update(extended, first_faces, 1)
            extended = jnp.concatenate([jnp.roll(fields, 1, axis=0)[:, :, SIDE - 3:], fields, jnp.roll(fields, -1, axis=0)[:, :, :3]], axis=2)
            fields = ppm_update(extended, second_faces, 2)
        advected = to_frame(fields, frame_flip)
        return jnp.einsum("txykl,txylq->txykq", mixing, advected, precision=lax.Precision.HIGHEST)

    grouped = tracers.reshape(TILES, SIDE, SIDE, LEVELS, TRACERS // group_width, group_width)
    grouped = jnp.moveaxis(grouped, 4, 0)
    results = lax.map(advance, grouped)
    return jnp.moveaxis(results, 0, 4).reshape(TILES, SIDE, SIDE, LEVELS, TRACERS)
```

```python
import jax
import jax.numpy as jnp
from jax import lax
from jax.experimental import pallas as pl
from jax.experimental.pallas import tpu as pltpu
from jax.sharding import PartitionSpec as P

MESH = pl.DeviceIdType.MESH
SUBSTEPS = 3
LEV = 18
CHUNKS = ((0, 8), (8, 4), (12, 6))
NCH = len(CHUNKS)


def swap_blocks(rows):
    lane = lax.broadcasted_iota(jnp.int32, (8, 128), 1)
    for m in (4, 2, 1):
        keep = (lane & (16 * m)) == 0
        fresh = list(rows)
        for k in range(8):
            if not k & m:
                a, b = rows[k], rows[k + m]
                fresh[k] = jnp.where(keep, a, pltpu.roll(b, 16 * m, 1))
                fresh[k + m] = jnp.where(keep, pltpu.roll(a, 128 - 16 * m, 1), b)
        rows = fresh
    return rows


def coefficients(c):
    up = c >= 0.0
    half = 0.5 * c * c
    b = half * (1.0 - jnp.abs(c) * (2.0 / 3.0))
    b = jnp.where(up, b, -b)
    signed = jnp.where(up, half, -half)
    return (c - signed - 3.0 * b) * (1.0 / 12.0), (signed - 3.0 * b) * (1.0 / 12.0), 6.0 * b


def face_value(q0, q1, q2, q3):
    return 7.0 * (q1 + q2) - (q0 + q3)


def face_flux(mid, below, above, q_below, q_above, ka, ku, kq):
    up = kq >= 0.0
    return ka * mid + ku * jnp.where(up, below, above) + kq * jnp.where(up, q_below, q_above)


def kernel(
    x_ref, c1_ref, c2_ref, w_ref, f_ref, o_ref,
    staged, send, recv, c_tmp, c_send, c_recv, raw, flags,
    fa, fb, halo_low, halo_high, edge_send, edge_recv,
    k1, k2, mix_send, mix_recv, columns, matrix, mixed,
    a_ssem, a_rsem, c_ssem, c_rsem, h_ssem, h_rsem, e_ssem, e_rsem, m_ssem, m_rsem, d_ssem, d_rsem, l_sem,
):
    t = lax.axis_index("tile")
    l = lax.axis_index("lev")
    ring = t // 8
    yc = t % 8
    hi = ring // 4
    x = ring % 4
    z = hi * 4 + l
    group = (l + 2) % 4
    eighth = (((z + 6) % 8) // 4) * 4 + x

    def at(zz, xx):
        return {"tile": ((zz // 4) * 4 + xx) * 8 + yc, "lev": zz % 4}

    low = {"tile": ring * 8 + (yc + 7) % 8, "lev": l}
    high = {"tile": ring * 8 + (yc + 1) % 8, "lev": l}

    barrier = pltpu.get_barrier_semaphore()

    def greet(o, carry):
        pl.semaphore_signal(barrier, inc=1, device_id=at((z + o // 4) % 8, (x + o % 4) % 4), device_id_type=MESH)
        return carry

    lax.fori_loop(1, 32, greet, 0)
    pl.semaphore_signal(barrier, inc=1, device_id=low, device_id_type=MESH)
    pl.semaphore_signal(barrier, inc=1, device_id=high, device_id_type=MESH)

    flip_i = f_ref[0, 0]
    flip_j = f_ref[0, 1]
    c_tmp[...] = jnp.zeros((128, 128), jnp.float32)
    for i in range(8):
        c_tmp[8 * i:8 * i + 8, 0:LEV] = c1_ref[0, i]
        c_tmp[64 + 8 * i:72 + 8 * i, 0:LEV] = c2_ref[0, i]
    turned = c_tmp[...].T
    c_send[...] = turned[0:24]
    c_send[18:19, :] = jnp.full((1, 128), flip_i, jnp.int32).astype(jnp.float32)
    c_send[19:20, :] = jnp.full((1, 128), flip_j, jnp.int32).astype(jnp.float32)

    def stage(i, carry):
        i2 = i + flip_i * (7 - 2 * i)
        for j in range(8):
            j2 = j + flip_j * (7 - 2 * j)
            staged[pl.ds(i * 8 + j, LEV, stride=64), :] = x_ref[0, i2, j2]
        return carry

    lax.fori_loop(0, 8, stage, 0)

    def pack(lev, carry):
        rows = [staged[pl.ds(pl.multiple_of(lev * 64 + 8 * i, 8), 8), :] for i in range(8)]
        rows = swap_blocks(rows)
        for d in range(8):
            send[d, lev] = rows[d]
        return carry

    lax.fori_loop(0, LEV, pack, 0)

    pl.semaphore_wait(barrier, 33)

    def target(d):
        return at((l + 2 + 4 * (d // 4)) % 8, d % 4)

    def c_copy(d, slot):
        return pltpu.make_async_remote_copy(
            src_ref=c_send, dst_ref=c_recv.at[pl.ds(slot * 24, 24)],
            send_sem=c_ssem.at[d], recv_sem=c_rsem.at[slot], device_id=target(d), device_id_type=MESH)

    def a_copy(d, slot, ch):
        first, count = CHUNKS[ch]
        return pltpu.make_async_remote_copy(
            src_ref=send.at[d, pl.ds(first, count)], dst_ref=recv.at[slot, pl.ds(first, count)],
            send_sem=a_ssem.at[d, ch], recv_sem=a_rsem.at[slot, ch], device_id=target(d), device_id_type=MESH)

    for d in range(8):
        c_copy(d, ring).start()
    for ch in range(NCH):
        for d in range(8):
            a_copy(d, ring, ch).start()

    def prepare(cell, carry):
        s, j = cell // 8, cell % 8
        for part in range(4):
            w = w_ref[0, s, j, 18 * part:18 * part + 18, :]
            same = lax.broadcasted_iota(jnp.int32, (18, 72), 1) == lax.broadcasted_iota(jnp.int32, (18, 72), 0) + 18 * part
            total = jnp.sum(w, axis=-1, keepdims=True)
            matrix[cell, 24 * part:24 * part + 18, :] = 0.4 * (w / total) + jnp.where(same, 0.6, 0.0)
        return carry

    lax.fori_loop(0, 16, prepare, 0)

    for slot in range(8):
        c_copy(slot, slot).wait_recv()
    spread = (
        lax.broadcasted_iota(jnp.int32, (24, 128), 0) % 8 == lax.broadcasted_iota(jnp.int32, (24, 128), 1) // 16
    ).astype(jnp.float32).astype(jnp.bfloat16)

    def spread_level(lev):
        v = c_recv[pl.ds(lev, 8, stride=24), :]
        p0 = v.astype(jnp.bfloat16).astype(jnp.float32)
        p1 = (v - p0).astype(jnp.bfloat16).astype(jnp.float32)
        p2 = v - p0 - p1
        parts = jnp.concatenate([p0, p1, p2], axis=0).astype(jnp.bfloat16)
        return lax.dot_general(parts, spread, (((0,), (0,)), ((), ())), preferred_element_type=jnp.float32)

    def courant(lev, carry):
        wide = spread_level(lev)
        for i in range(8):
            for n, value in enumerate(coefficients(wide[8 * i:8 * i + 8])):
                k1[n, lev, 8 * i:8 * i + 8, :] = value
            raw[pl.ds(i, 8, stride=8), :] = wide[64 + 8 * i:72 + 8 * i]
        for j in range(8):
            for n, value in enumerate(coefficients(raw[8 * j:8 * j + 8, :])):
                k2[n, lev, 8 * j + 8:8 * j + 16, :] = value
        edge_send[lev] = raw[56:64, :]
        return carry

    lax.fori_loop(0, LEV, courant, 0)
    for n in range(2):
        flags[n] = spread_level(18 + n)[0:8]

    edge = pltpu.make_async_remote_copy(
        src_ref=edge_send, dst_ref=edge_recv, send_sem=e_ssem, recv_sem=e_rsem, device_id=high, device_id_type=MESH)
    edge.start()

    roll_low = jnp.where(yc == 0, 16, 0)
    roll_high = jnp.where(yc == 7, 112, 0)

    def unpack(ch):
        first, count = CHUNKS[ch]
        for slot in range(8):
            a_copy(slot, slot, ch).wait_recv()

        def one(lev, carry):
            rows = swap_blocks([recv[slot, lev] for slot in range(8)])
            for i in range(8):
                fa[lev, 8 * i:8 * i + 8, :] = rows[i]
            return carry

        lax.fori_loop(first, first + count, one, 0)

    def sweep_first(step, ch):
        first, count = CHUNKS[ch]

        def one(lev, carry):
            q = [fa[lev, 8 * i:8 * i + 8, :] for i in range(8)]
            e = [pltpu.roll(q[7], 16, 1)] + q + [pltpu.roll(q[0], 112, 1), pltpu.roll(q[1], 112, 1)]
            a = [face_value(*e[i:i + 4]) for i in range(8)]
            a = [pltpu.roll(a[7], 16, 1)] + a + [pltpu.roll(a[0], 112, 1)]
            flux = []
            for i in range(8):
                k = [k1[n, lev, 8 * i:8 * i + 8, :] for n in range(3)]
                flux.append(face_flux(a[i + 1], a[i], a[i + 2], e[i + 1], e[i + 2], *k))
            flux = [pltpu.roll(flux[7], 16, 1)] + flux
            for i in range(8):
                fb[step, lev, pl.ds(i, 8, stride=8), :] = q[i] - (flux[i + 1] - flux[i])
            return carry

        lax.fori_loop(first, first + count, one, 0)

    def halo_copies(step, ch):
        first, count = CHUNKS[ch]
        return (
            pltpu.make_async_remote_copy(
                src_ref=fb.at[step, pl.ds(first, count), pl.ds(40, 24)], dst_ref=halo_low.at[step, pl.ds(first, count)],
                send_sem=h_ssem.at[0, step, ch], recv_sem=h_rsem.at[0, step, ch], device_id=high, device_id_type=MESH),
            pltpu.make_async_remote_copy(
                src_ref=fb.at[step, pl.ds(first, count), pl.ds(0, 24)], dst_ref=halo_high.at[step, pl.ds(first, count)],
                send_sem=h_ssem.at[1, step, ch], recv_sem=h_rsem.at[1, step, ch], device_id=low, device_id_type=MESH),
        )

    def sweep_second(step, ch):
        first, count = CHUNKS[ch]
        last = step == SUBSTEPS - 1

        def one(lev, carry):
            q = [fb[step, lev, 8 * j:8 * j + 8, :] for j in range(8)]
            e = [pltpu.roll(halo_low[step, lev, 8 * j:8 * j + 8, :], roll_low, 1) for j in range(3)] + q
            e += [pltpu.roll(halo_high[step, lev, 8 * j:8 * j + 8, :], roll_high, 1) for j in range(3)]
            a = [face_value(*e[k:k + 4]) for k in range(11)]
            flux = []
            for f in range(9):
                k = [k2[n, lev, 8 * f:8 * f + 8, :] for n in range(3)]
                flux.append(face_flux(a[f + 1], a[f], a[f + 2], e[f + 2], e[f + 3], *k))
            new = [q[j] - (flux[j + 1] - flux[j]) for j in range(8)]
            if last:
                back = flags[1] > 0.5
                new = [jnp.where(back, new[7 - j], new[j]) for j in range(8)]
            for j in range(8):
                fa[lev, pl.ds(j, 8, stride=8), :] = new[j]
            return carry

        lax.fori_loop(first, first + count, one, 0)

    for ch in range(NCH):
        unpack(ch)
        sweep_first(0, ch)
        for copy in halo_copies(0, ch):
            copy.start()

    edge.wait_recv()

    def edge_level(lev, carry):
        for n, value in enumerate(coefficients(pltpu.roll(edge_recv[lev], roll_low, 1))):
            k2[n, lev, 0:8, :] = value
        return carry

    lax.fori_loop(0, LEV, edge_level, 0)

    for step in range(SUBSTEPS):
        for ch in range(NCH):
            for copy in halo_copies(step, ch):
                copy.wait_recv()
            sweep_second(step, ch)
            if step < SUBSTEPS - 1:
                sweep_first(step + 1, ch)
                for copy in halo_copies(step + 1, ch):
                    copy.start()

    def mix_pack(r, carry):
        back = flags[0] > 0.5
        for m in range(5):
            rows = []
            for k in range(8):
                lev, i = 4 * m + k // 2, 2 * r + k % 2
                if lev < LEV:
                    here = fa[lev, pl.ds(pl.multiple_of(8 * i, 8), 8), :]
                    there = fa[lev, pl.ds(pl.multiple_of(56 - 8 * i, 8), 8), :]
                    rows.append(jnp.where(back, there, here))
                else:
                    rows.append(jnp.zeros((8, 128), jnp.float32))
            rows = swap_blocks(rows)
            for k in range(8):
                mix_send[k * 4 + r, m] = rows[k]
        return carry

    lax.fori_loop(0, 4, mix_pack, 0)

    def m_copy(o):
        zd, xd = (z + o // 4) % 8, (x + o % 4) % 4
        return pltpu.make_async_remote_copy(
            src_ref=mix_send.at[((zd // 4) * 4 + xd) * 4 + zd % 4], dst_ref=mix_recv.at[group * 8 + eighth],
            send_sem=m_ssem.at[o], recv_sem=m_rsem.at[o], device_id=at(zd, xd), device_id_type=MESH)

    def m_arrival(o):
        zs, xs = (z + 8 - o // 4) % 8, (x + 4 - o % 4) % 4
        slot = ((zs + 2) % 4) * 8 + (((zs + 6) % 8) // 4) * 4 + xs
        return pltpu.make_async_remote_copy(
            src_ref=mix_send.at[0], dst_ref=mix_recv.at[slot],
            send_sem=m_ssem.at[o], recv_sem=m_rsem.at[o], device_id=at(zs, xs), device_id_type=MESH)

    def m_start(o, carry):
        m_copy(o).start()
        return carry

    lax.fori_loop(1, 32, m_start, 0)
    own = pltpu.make_async_copy(mix_send.at[ring * 4 + l], mix_recv.at[group * 8 + eighth], l_sem.at[0])
    own.start()

    def m_wait(o, carry):
        m_arrival(o).wait_recv()
        return carry

    lax.fori_loop(1, 32, m_wait, 0)
    own.wait()

    def mix_unpack(g, carry):
        for m in range(5):
            rows = swap_blocks([mix_recv[g * 8 + k, m] for k in range(8)])
            for k in range(8):
                lev, s = 4 * m + k // 2, k % 2
                if lev < LEV:
                    columns[s, pl.ds(pl.multiple_of((g * LEV + lev) * 8, 8), 8), :] = rows[k]
        return carry

    lax.fori_loop(0, 4, mix_unpack, 0)

    def d_copy(s, o):
        to = (l + o) % 4
        return pltpu.make_async_remote_copy(
            src_ref=mixed.at[s, to], dst_ref=o_ref.at[0, 2 * l + s],
            send_sem=d_ssem.at[s, o], recv_sem=d_rsem.at[s, o], device_id={"tile": t, "lev": to}, device_id_type=MESH)

    def d_arrival(s, o):
        source = (l + 4 - o) % 4
        return pltpu.make_async_remote_copy(
            src_ref=mixed.at[s, 0], dst_ref=o_ref.at[0, 2 * source + s],
            send_sem=d_ssem.at[s, o], recv_sem=d_rsem.at[s, o], device_id={"tile": t, "lev": source}, device_id_type=MESH)

    def mix_row(s):
        def one(j, carry):
            v = columns[s, pl.ds(j, 72, stride=8), :]
            v_hi = v.astype(jnp.bfloat16)
            v_lo = (v - v_hi.astype(jnp.float32)).astype(jnp.bfloat16)
            m = matrix[s * 8 + j]
            m_hi = m.astype(jnp.bfloat16)
            m_lo = (m - m_hi.astype(jnp.float32)).astype(jnp.bfloat16)
            dot = lambda a, b: jnp.dot(a, b, preferred_element_type=jnp.float32)
            out = dot(m_hi, v_hi) + (dot(m_hi, v_lo) + dot(m_lo, v_hi))
            for part in range(4):
                mixed[s, part, j] = out[24 * part:24 * part + 18]
            return carry

        lax.fori_loop(0, 8, one, 0)

    local = []
    for s in range(2):
        mix_row(s)
        for o in range(1, 4):
            d_copy(s, o).start()
        local.append(pltpu.make_async_copy(mixed.at[s, l], o_ref.at[0, 2 * l + s], l_sem.at[1 + s]))
        local[s].start()

    for d in range(8):
        c_copy(d, ring).wait_send()
        for ch in range(NCH):
            a_copy(d, ring, ch).wait_send()
    edge.wait_send()
    for step in range(SUBSTEPS):
        for ch in range(NCH):
            for copy in halo_copies(step, ch):
                copy.wait_send()

    def m_end(o, carry):
        m_copy(o).wait_send()
        return carry

    lax.fori_loop(1, 32, m_end, 0)
    for s in range(2):
        for o in range(1, 4):
            d_copy(s, o).wait_send()
            d_arrival(s, o).wait_recv()
        local[s].wait()


def solution(mesh):
    f32 = jnp.float32

    def on_device(tracers, courant_first, courant_second, weights, frame_flip):
        vmem = pl.BlockSpec(memory_space=pltpu.VMEM)
        dma = pltpu.SemaphoreType.DMA
        return pl.pallas_call(
            kernel,
            out_shape=jax.ShapeDtypeStruct(tracers.shape, f32),
            in_specs=[vmem, vmem, vmem, vmem, pl.BlockSpec(memory_space=pltpu.SMEM)],
            out_specs=vmem,
            scratch_shapes=[
                pltpu.VMEM((LEV * 64, 128), f32),
                pltpu.VMEM((8, LEV, 8, 128), f32),
                pltpu.VMEM((8, LEV, 8, 128), f32),
                pltpu.VMEM((128, 128), f32),
                pltpu.VMEM((24, 128), f32),
                pltpu.VMEM((192, 128), f32),
                pltpu.VMEM((64, 128), f32),
                pltpu.VMEM((2, 8, 128), f32),
                pltpu.VMEM((LEV, 64, 128), f32),
                pltpu.VMEM((SUBSTEPS, LEV, 64, 128), f32),
                pltpu.VMEM((SUBSTEPS, LEV, 24, 128), f32),
                pltpu.VMEM((SUBSTEPS, LEV, 24, 128), f32),
                pltpu.VMEM((LEV, 8, 128), f32),
                pltpu.VMEM((LEV, 8, 128), f32),
                pltpu.VMEM((3, LEV, 64, 128), f32),
                pltpu.VMEM((3, LEV, 72, 128), f32),
                pltpu.VMEM((32, 5, 8, 128), f32),
                pltpu.VMEM((32, 5, 8, 128), f32),
                pltpu.VMEM((2, 72 * 8, 128), f32),
                pltpu.VMEM((16, 96, 72), f32),
                pltpu.VMEM((2, 4, 8, LEV, 128), f32),
                dma((8, NCH)), dma((8, NCH)),
                dma((8,)), dma((8,)),
                dma((2, SUBSTEPS, NCH)), dma((2, SUBSTEPS, NCH)),
                dma, dma,
                dma((32,)), dma((32,)),
                dma((2, 4)), dma((2, 4)),
                dma((3,)),
            ],
            compiler_params=pltpu.CompilerParams(collective_id=0, has_side_effects=True),
        )(tracers, courant_first, courant_second, weights, frame_flip)

    return jax.shard_map(
        on_device,
        mesh=mesh,
        in_specs=(
            P("tile", None, None, "lev", None),
            P("tile", None, None, "lev"),
            P("tile", None, None, "lev"),
            P("tile", "lev", None, None, None),
            P("tile", None),
        ),
        out_specs=P("tile", None, None, "lev", None),
        check_vma=False,
    )
```

```python
import jax
import jax.numpy as jnp
from jax import lax
from jax.experimental import pallas as pl
from jax.experimental.pallas import tpu as pltpu
from jax.sharding import PartitionSpec as P

MESH = pl.DeviceIdType.MESH
SUBSTEPS = 3
LEV = 18
CHUNKS = ((0, 8), (8, 4), (12, 6))
NCH = len(CHUNKS)
UNROLL = 2


def swap_blocks(rows):
    lane = lax.broadcasted_iota(jnp.int32, (8, 128), 1)
    for m in (4, 2, 1):
        keep = (lane & (16 * m)) == 0
        fresh = list(rows)
        for k in range(8):
            if not k & m:
                a, b = rows[k], rows[k + m]
                fresh[k] = jnp.where(keep, a, pltpu.roll(b, 16 * m, 1))
                fresh[k + m] = jnp.where(keep, pltpu.roll(a, 128 - 16 * m, 1), b)
        rows = fresh
    return rows


def reverse_rows(v):
    row = lax.broadcasted_iota(jnp.int32, (8, 128), 0)
    v = pltpu.roll(v, 4, 0)
    v = jnp.where((row & 2) == 0, pltpu.roll(v, 6, 0), pltpu.roll(v, 2, 0))
    return jnp.where((row & 1) == 0, pltpu.roll(v, 7, 0), pltpu.roll(v, 1, 0))


def coefficients(c):
    up = c >= 0.0
    half = 0.5 * c * c
    b = half * (1.0 - jnp.abs(c) * (2.0 / 3.0))
    b = jnp.where(up, b, -b)
    signed = jnp.where(up, half, -half)
    return (c - signed - 3.0 * b) * (1.0 / 12.0), (signed - 3.0 * b) * (1.0 / 12.0), 6.0 * b


def face_value(q0, q1, q2, q3):
    return 7.0 * (q1 + q2) - (q0 + q3)


def face_flux(mid, below, above, q_below, q_above, ka, ku, kq):
    up = kq >= 0.0
    return ka * mid + ku * jnp.where(up, below, above) + kq * jnp.where(up, q_below, q_above)


def kernel(
    x_ref, c1_ref, c2_ref, w_ref, f_ref, o_ref,
    x_vmem, w_vmem, send, recv, c_tmp, c_send, c_recv, raw, flags,
    fa, fb, halo_low, halo_high, edge_send, edge_recv,
    k1, k2, mix_send, mix_recv, columns, matrix, mixed,
    a_ssem, a_rsem, c_ssem, c_rsem, h_ssem, h_rsem, e_ssem, e_rsem, m_ssem, m_rsem, d_ssem, d_rsem, l_sem, i_sem,
):
    t = lax.axis_index("tile")
    l = lax.axis_index("lev")
    ring = t // 8
    yc = t % 8
    hi = ring // 4
    x = ring % 4
    z = hi * 4 + l
    group = (l + 2) % 4
    eighth = (((z + 6) % 8) // 4) * 4 + x

    def at(zz, xx):
        return {"tile": ((zz // 4) * 4 + xx) * 8 + yc, "lev": zz % 4}

    low = {"tile": ring * 8 + (yc + 7) % 8, "lev": l}
    high = {"tile": ring * 8 + (yc + 1) % 8, "lev": l}

    barrier = pltpu.get_barrier_semaphore()
    greeted = [at((z + dz) % 8, (x + dx) % 4) for dz in (2, 6) for dx in range(4)]
    greeted += [at((z + 1) % 8, x), at((z + 7) % 8, x), low, high]
    for device in greeted:
        pl.semaphore_signal(barrier, inc=1, device_id=device, device_id_type=MESH)
    x_load = pltpu.make_async_copy(x_ref.at[0], x_vmem, i_sem.at[0])
    w_load = pltpu.make_async_copy(w_ref.at[0], w_vmem, i_sem.at[1])
    x_load.start()
    w_load.start()

    flip_i = f_ref[0, 0]
    flip_j = f_ref[0, 1]
    c_tmp[...] = jnp.zeros((128, 128), jnp.float32)
    for i in range(8):
        c_tmp[8 * i:8 * i + 8, 0:LEV] = c1_ref[0, i]
        c_tmp[64 + 8 * i:72 + 8 * i, 0:LEV] = c2_ref[0, i]
    turned = c_tmp[...].T
    c_send[...] = turned[0:24]
    c_send[18:19, :] = jnp.full((1, 128), flip_i, jnp.int32).astype(jnp.float32)
    c_send[19:20, :] = jnp.full((1, 128), flip_j, jnp.int32).astype(jnp.float32)

    x_load.wait()
    turn = jnp.full((8, 128), flip_j, jnp.int32) == 1

    def pack(lev, carry):
        rows = [x_vmem[i + flip_i * (7 - 2 * i), lev] for i in range(8)]
        rows = swap_blocks([jnp.where(turn, reverse_rows(v), v) for v in rows])
        for d in range(8):
            send[d, lev] = rows[d]
        return carry

    lax.fori_loop(0, LEV, pack, 0)

    pl.semaphore_wait(barrier, len(greeted))

    def target(d):
        return at((l + 2 + 4 * (d // 4)) % 8, d % 4)

    def c_copy(d, slot):
        return pltpu.make_async_remote_copy(
            src_ref=c_send, dst_ref=c_recv.at[pl.ds(slot * 24, 24)],
            send_sem=c_ssem.at[d], recv_sem=c_rsem.at[slot], device_id=target(d), device_id_type=MESH)

    def a_copy(d, slot, ch):
        first, count = CHUNKS[ch]
        return pltpu.make_async_remote_copy(
            src_ref=send.at[d, pl.ds(first, count)], dst_ref=recv.at[slot, pl.ds(first, count)],
            send_sem=a_ssem.at[d, ch], recv_sem=a_rsem.at[slot, ch], device_id=target(d), device_id_type=MESH)

    for d in range(8):
        c_copy(d, ring).start()
    for ch in range(NCH):
        for d in range(8):
            a_copy(d, ring, ch).start()

    w_load.wait()
    diagonal = jnp.where(
        lax.broadcasted_iota(jnp.int32, (72, 72), 0) == lax.broadcasted_iota(jnp.int32, (72, 72), 1), 0.6, 0.0)

    def prepare(cell, carry):
        s, j = cell // 8, cell % 8
        w = w_vmem[s, j]
        total = jnp.sum(w, axis=-1, keepdims=True)
        matrix[cell] = 0.4 * (w / total) + diagonal
        return carry

    lax.fori_loop(0, 16, prepare, 0)

    for slot in range(8):
        c_copy(slot, slot).wait_recv()
    spread = (
        lax.broadcasted_iota(jnp.int32, (24, 128), 0) % 8 == lax.broadcasted_iota(jnp.int32, (24, 128), 1) // 16
    ).astype(jnp.float32).astype(jnp.bfloat16)

    def spread_level(lev):
        v = c_recv[pl.ds(lev, 8, stride=24), :]
        p0 = v.astype(jnp.bfloat16).astype(jnp.float32)
        p1 = (v - p0).astype(jnp.bfloat16).astype(jnp.float32)
        p2 = v - p0 - p1
        parts = jnp.concatenate([p0, p1, p2], axis=0).astype(jnp.bfloat16)
        return lax.dot_general(parts, spread, (((0,), (0,)), ((), ())), preferred_element_type=jnp.float32)

    def courant(lev, carry):
        wide = spread_level(lev)
        for i in range(8):
            for n, value in enumerate(coefficients(wide[8 * i:8 * i + 8])):
                k1[n, lev, 8 * i:8 * i + 8, :] = value
            raw[pl.ds(i, 8, stride=8), :] = wide[64 + 8 * i:72 + 8 * i]
        for j in range(8):
            for n, value in enumerate(coefficients(raw[8 * j:8 * j + 8, :])):
                k2[n, lev, 8 * j + 8:8 * j + 16, :] = value
        edge_send[lev] = raw[56:64, :]
        return carry

    lax.fori_loop(0, LEV, courant, 0)
    for n in range(2):
        flags[n] = spread_level(18 + n)[0:8]

    edge = pltpu.make_async_remote_copy(
        src_ref=edge_send, dst_ref=edge_recv, send_sem=e_ssem, recv_sem=e_rsem, device_id=high, device_id_type=MESH)
    edge.start()

    roll_low = jnp.where(yc == 0, 16, 0)
    roll_high = jnp.where(yc == 7, 112, 0)

    def unpack(ch):
        first, count = CHUNKS[ch]
        for slot in range(8):
            a_copy(slot, slot, ch).wait_recv()

        def one(lev, carry):
            rows = swap_blocks([recv[slot, lev] for slot in range(8)])
            for i in range(8):
                fa[lev, 8 * i:8 * i + 8, :] = rows[i]
            return carry

        lax.fori_loop(first, first + count, one, 0)

    def sweep_first(step, ch):
        first, count = CHUNKS[ch]

        def level(lev):
            q = [fa[lev, 8 * i:8 * i + 8, :] for i in range(8)]
            e = [pltpu.roll(q[7], 16, 1)] + q + [pltpu.roll(q[0], 112, 1), pltpu.roll(q[1], 112, 1)]
            a = [face_value(*e[i:i + 4]) for i in range(8)]
            a = [pltpu.roll(a[7], 16, 1)] + a + [pltpu.roll(a[0], 112, 1)]
            flux = []
            for i in range(8):
                k = [k1[n, lev, 8 * i:8 * i + 8, :] for n in range(3)]
                flux.append(face_flux(a[i + 1], a[i], a[i + 2], e[i + 1], e[i + 2], *k))
            flux = [pltpu.roll(flux[7], 16, 1)] + flux
            return [q[i] - (flux[i + 1] - flux[i]) for i in range(8)]

        def some(n, carry):
            levels = [first + n * UNROLL + k for k in range(UNROLL)]
            new = [level(lev) for lev in levels]
            for lev, rows in zip(levels, new):
                for i in range(8):
                    fb[step, lev, pl.ds(i, 8, stride=8), :] = rows[i]
            return carry

        lax.fori_loop(0, count // UNROLL, some, 0)

    def halo_copies(step, ch):
        first, count = CHUNKS[ch]
        return (
            pltpu.make_async_remote_copy(
                src_ref=fb.at[step, pl.ds(first, count), pl.ds(40, 24)], dst_ref=halo_low.at[step, pl.ds(first, count)],
                send_sem=h_ssem.at[0, step, ch], recv_sem=h_rsem.at[0, step, ch], device_id=high, device_id_type=MESH),
            pltpu.make_async_remote_copy(
                src_ref=fb.at[step, pl.ds(first, count), pl.ds(0, 24)], dst_ref=halo_high.at[step, pl.ds(first, count)],
                send_sem=h_ssem.at[1, step, ch], recv_sem=h_rsem.at[1, step, ch], device_id=low, device_id_type=MESH),
        )

    def sweep_second(step, ch):
        first, count = CHUNKS[ch]
        last = step == SUBSTEPS - 1

        def level(lev):
            q = [fb[step, lev, 8 * j:8 * j + 8, :] for j in range(8)]
            e = [pltpu.roll(halo_low[step, lev, 8 * j:8 * j + 8, :], roll_low, 1) for j in range(3)] + q
            e += [pltpu.roll(halo_high[step, lev, 8 * j:8 * j + 8, :], roll_high, 1) for j in range(3)]
            a = [face_value(*e[k:k + 4]) for k in range(11)]
            flux = []
            for f in range(9):
                k = [k2[n, lev, 8 * f:8 * f + 8, :] for n in range(3)]
                flux.append(face_flux(a[f + 1], a[f], a[f + 2], e[f + 2], e[f + 3], *k))
            new = [q[j] - (flux[j + 1] - flux[j]) for j in range(8)]
            if last:
                back = flags[1] > 0.5
                new = [jnp.where(back, new[7 - j], new[j]) for j in range(8)]
            return new

        def some(n, carry):
            levels = [first + n * UNROLL + k for k in range(UNROLL)]
            new = [level(lev) for lev in levels]
            for lev, rows in zip(levels, new):
                for j in range(8):
                    fa[lev, pl.ds(j, 8, stride=8), :] = rows[j]
            return carry

        lax.fori_loop(0, count // UNROLL, some, 0)

    for ch in range(NCH):
        unpack(ch)
        sweep_first(0, ch)
        for copy in halo_copies(0, ch):
            copy.start()

    edge.wait_recv()

    def edge_level(lev, carry):
        for n, value in enumerate(coefficients(pltpu.roll(edge_recv[lev], roll_low, 1))):
            k2[n, lev, 0:8, :] = value
        return carry

    lax.fori_loop(0, LEV, edge_level, 0)

    for step in range(SUBSTEPS):
        for ch in range(NCH):
            for copy in halo_copies(step, ch):
                copy.wait_recv()
            sweep_second(step, ch)
            if step < SUBSTEPS - 1:
                sweep_first(step + 1, ch)
                for copy in halo_copies(step + 1, ch):
                    copy.start()

    def mix_pack(r, carry):
        back = flags[0] > 0.5
        for m in range(5):
            rows = []
            for k in range(8):
                lev, i = 4 * m + k // 2, 2 * r + k % 2
                if lev < LEV:
                    here = fa[lev, pl.ds(pl.multiple_of(8 * i, 8), 8), :]
                    there = fa[lev, pl.ds(pl.multiple_of(56 - 8 * i, 8), 8), :]
                    rows.append(jnp.where(back, there, here))
                else:
                    rows.append(jnp.zeros((8, 128), jnp.float32))
            rows = swap_blocks(rows)
            for k in range(8):
                mix_send[k * 4 + r, m] = rows[k]
        return carry

    lax.fori_loop(0, 4, mix_pack, 0)

    def m_copy(o):
        zd, xd = (z + o // 4) % 8, (x + o % 4) % 4
        return pltpu.make_async_remote_copy(
            src_ref=mix_send.at[((zd // 4) * 4 + xd) * 4 + zd % 4], dst_ref=mix_recv.at[group * 8 + eighth],
            send_sem=m_ssem.at[o], recv_sem=m_rsem.at[o], device_id=at(zd, xd), device_id_type=MESH)

    def m_arrival(o):
        zs, xs = (z + 8 - o // 4) % 8, (x + 4 - o % 4) % 4
        slot = ((zs + 2) % 4) * 8 + (((zs + 6) % 8) // 4) * 4 + xs
        return pltpu.make_async_remote_copy(
            src_ref=mix_send.at[0], dst_ref=mix_recv.at[slot],
            send_sem=m_ssem.at[o], recv_sem=m_rsem.at[o], device_id=at(zs, xs), device_id_type=MESH)

    def m_start(o, carry):
        m_copy(o).start()
        return carry

    lax.fori_loop(1, 32, m_start, 0)
    own = pltpu.make_async_copy(mix_send.at[ring * 4 + l], mix_recv.at[group * 8 + eighth], l_sem.at[0])
    own.start()

    def m_wait(o, carry):
        m_arrival(o).wait_recv()
        return carry

    lax.fori_loop(1, 32, m_wait, 0)
    own.wait()

    def mix_unpack(g, carry):
        for m in range(5):
            rows = swap_blocks([mix_recv[g * 8 + k, m] for k in range(8)])
            for k in range(8):
                lev, s = 4 * m + k // 2, k % 2
                if lev < LEV:
                    columns[s, pl.ds(pl.multiple_of((g * LEV + lev) * 8, 8), 8), :] = rows[k]
        return carry

    lax.fori_loop(0, 4, mix_unpack, 0)

    def d_copy(s, o):
        to = (l + o) % 4
        return pltpu.make_async_remote_copy(
            src_ref=mixed.at[s, pl.ds(to * 144, 144)], dst_ref=o_ref.at[0, 2 * l + s],
            send_sem=d_ssem.at[s, o], recv_sem=d_rsem.at[s, o], device_id={"tile": t, "lev": to}, device_id_type=MESH)

    def d_arrival(s, o):
        source = (l + 4 - o) % 4
        return pltpu.make_async_remote_copy(
            src_ref=mixed.at[s, pl.ds(0, 144)], dst_ref=o_ref.at[0, 2 * source + s],
            send_sem=d_ssem.at[s, o], recv_sem=d_rsem.at[s, o], device_id={"tile": t, "lev": source}, device_id_type=MESH)

    def mix_row(s):
        def one(j, carry):
            v = columns[s, pl.ds(j, 72, stride=8), :]
            v_hi = v.astype(jnp.bfloat16)
            v_lo = (v - v_hi.astype(jnp.float32)).astype(jnp.bfloat16)
            m = matrix[s * 8 + j]
            m_hi = m.astype(jnp.bfloat16)
            m_lo = (m - m_hi.astype(jnp.float32)).astype(jnp.bfloat16)
            dot = lambda a, b: jnp.dot(a, b, preferred_element_type=jnp.float32)
            out = dot(m_hi, v_hi) + (dot(m_hi, v_lo) + dot(m_lo, v_hi))
            mixed[s, pl.ds(j, 72, stride=8), :] = out
            return carry

        lax.fori_loop(0, 8, one, 0)

    local = []
    for s in range(2):
        mix_row(s)
        for o in range(1, 4):
            d_copy(s, o).start()
        local.append(pltpu.make_async_copy(mixed.at[s, pl.ds(l * 144, 144)], o_ref.at[0, 2 * l + s], l_sem.at[1 + s]))
        local[s].start()

    for d in range(8):
        c_copy(d, ring).wait_send()
        for ch in range(NCH):
            a_copy(d, ring, ch).wait_send()
    edge.wait_send()
    for step in range(SUBSTEPS):
        for ch in range(NCH):
            for copy in halo_copies(step, ch):
                copy.wait_send()

    def m_end(o, carry):
        m_copy(o).wait_send()
        return carry

    lax.fori_loop(1, 32, m_end, 0)
    for s in range(2):
        for o in range(1, 4):
            d_copy(s, o).wait_send()
            d_arrival(s, o).wait_recv()
        local[s].wait()


def solution(mesh):
    f32 = jnp.float32

    def on_device(tracers, courant_first, courant_second, weights, frame_flip):
        vmem = pl.BlockSpec(memory_space=pltpu.VMEM)
        hbm = pl.BlockSpec(memory_space=pl.ANY)
        dma = pltpu.SemaphoreType.DMA
        rows = jnp.transpose(tracers, (0, 1, 3, 2, 4)).reshape(1, 8, LEV, 8, 128)
        out = pl.pallas_call(
            kernel,
            out_shape=jax.ShapeDtypeStruct((1, 8, LEV * 8, 128), f32),
            in_specs=[hbm, vmem, vmem, hbm, pl.BlockSpec(memory_space=pltpu.SMEM)],
            out_specs=vmem,
            scratch_shapes=[
                pltpu.VMEM((8, LEV, 8, 128), f32),
                pltpu.VMEM((2, 8, 72, 72), f32),
                pltpu.VMEM((8, LEV, 8, 128), f32),
                pltpu.VMEM((8, LEV, 8, 128), f32),
                pltpu.VMEM((128, 128), f32),
                pltpu.VMEM((24, 128), f32),
                pltpu.VMEM((192, 128), f32),
                pltpu.VMEM((64, 128), f32),
                pltpu.VMEM((2, 8, 128), f32),
                pltpu.VMEM((LEV, 64, 128), f32),
                pltpu.VMEM((SUBSTEPS, LEV, 64, 128), f32),
                pltpu.VMEM((SUBSTEPS, LEV, 24, 128), f32),
                pltpu.VMEM((SUBSTEPS, LEV, 24, 128), f32),
                pltpu.VMEM((LEV, 8, 128), f32),
                pltpu.VMEM((LEV, 8, 128), f32),
                pltpu.VMEM((3, LEV, 64, 128), f32),
                pltpu.VMEM((3, LEV, 72, 128), f32),
                pltpu.VMEM((32, 5, 8, 128), f32),
                pltpu.VMEM((32, 5, 8, 128), f32),
                pltpu.VMEM((2, 72 * 8, 128), f32),
                pltpu.VMEM((16, 72, 72), f32),
                pltpu.VMEM((2, 72 * 8, 128), f32),
                dma((8, NCH)), dma((8, NCH)),
                dma((8,)), dma((8,)),
                dma((2, SUBSTEPS, NCH)), dma((2, SUBSTEPS, NCH)),
                dma, dma,
                dma((32,)), dma((32,)),
                dma((2, 4)), dma((2, 4)),
                dma((3,)),
                dma((2,)),
            ],
            compiler_params=pltpu.CompilerParams(collective_id=0, has_side_effects=True),
        )(rows, courant_first, courant_second, weights, frame_flip)
        return jnp.transpose(out.reshape(1, 8, LEV, 8, 128), (0, 1, 3, 2, 4))

    return jax.shard_map(
        on_device,
        mesh=mesh,
        in_specs=(
            P("tile", None, None, "lev", None),
            P("tile", None, None, "lev"),
            P("tile", None, None, "lev"),
            P("tile", "lev", None, None, None),
            P("tile", None),
        ),
        out_specs=P("tile", None, None, "lev", None),
        check_vma=False,
    )
```

```python
import jax
import jax.numpy as jnp
from jax import lax
from jax.experimental import pallas as pl
from jax.experimental.pallas import tpu as pltpu
from jax.sharding import PartitionSpec as P

MESH = pl.DeviceIdType.MESH
SUBSTEPS = 3
LEV = 18
CHUNKS = ((0, 8), (8, 4), (12, 6))
NCH = len(CHUNKS)
GROUPS = tuple(tuple(range(first // 4, (first + count + 3) // 4)) for first, count in CHUNKS)
UNROLL = 2


def turn_blocks(rows):
    return [pltpu.roll(v, 16 * k, 1) if k else v for k, v in enumerate(rows)]


def pick_blocks(rows):
    block = lax.broadcasted_iota(jnp.int32, (8, 128), 1) // 16
    rows = [rows[(8 - b) % 8] for b in range(8)]
    for m in (1, 2, 4):
        other = (block & m) != 0
        rows = [jnp.where(other, rows[(b + 8 - m) % 8], rows[b]) for b in range(8)]
    return rows


def turn_back(rows):
    return [pltpu.roll(v, 128 - 16 * b, 1) if b else v for b, v in enumerate(rows)]


def coefficients(c):
    up = c >= 0.0
    half = 0.5 * c * c
    b = half * (1.0 - jnp.abs(c) * (2.0 / 3.0))
    b = jnp.where(up, b, -b)
    signed = jnp.where(up, half, -half)
    return (c - signed - 3.0 * b) * (1.0 / 12.0), (signed - 3.0 * b) * (1.0 / 12.0), 6.0 * b


def face_value(q0, q1, q2, q3):
    return 7.0 * (q1 + q2) - (q0 + q3)


def face_flux(mid, below, above, q_below, q_above, ka, ku, kq):
    up = kq >= 0.0
    return ka * mid + ku * jnp.where(up, below, above) + kq * jnp.where(up, q_below, q_above)


def kernel(
    x_ref, c1_ref, c2_ref, w_ref, f_ref, o_ref,
    x_vmem, w_vmem, send, recv, c_tmp, c_send, c_recv, raw, flags,
    fa, fb, halo_low, halo_high, edge_send, edge_recv,
    k1, k2, mix_send, mix_recv, columns, matrix, mixed,
    a_ssem, a_rsem, c_ssem, c_rsem, h_ssem, h_rsem, e_ssem, e_rsem, m_ssem, m_rsem, d_ssem, d_rsem, l_sem, i_sem,
):
    t = lax.axis_index("tile")
    l = lax.axis_index("lev")
    div, rem = lax.div, lax.rem
    ring = div(t, 8)
    yc = rem(t, 8)
    hi = div(ring, 4)
    x = rem(ring, 4)
    z = hi * 4 + l
    group = rem(l + 2, 4)
    eighth = div(rem(z + 6, 8), 4) * 4 + x

    def at(zz, xx):
        return {"tile": (div(zz, 4) * 4 + xx) * 8 + yc, "lev": rem(zz, 4)}

    low = {"tile": ring * 8 + rem(yc + 7, 8), "lev": l}
    high = {"tile": ring * 8 + rem(yc + 1, 8), "lev": l}

    pending = {}

    def begin(key, start, sent, arrived):
        start()
        pending[key] = [arrived, sent]

    def left(*keys):
        for key in keys:
            pending[key][1]()
            pending[key][1] = lambda: None

    def arrive(*keys):
        for key in keys:
            pending[key][0]()
            pending[key][0] = None

    barrier = pltpu.get_barrier_semaphore()
    greeted = [at(rem(z + dz, 8), rem(x + dx, 4)) for dz in (2, 6) for dx in range(4)]
    greeted += [at(rem(z + 1, 8), x), at(rem(z + 7, 8), x), low, high]
    for device in greeted:
        pl.semaphore_signal(barrier, inc=1, device_id=device, device_id_type=MESH)
    x_load = pltpu.make_async_copy(x_ref.at[0], x_vmem, i_sem.at[0])
    w_load = pltpu.make_async_copy(w_ref.at[0], w_vmem, i_sem.at[1])
    x_load.start()
    w_load.start()

    flip_i = f_ref[0, 0]
    flip_j = f_ref[0, 1]
    c_tmp[...] = jnp.zeros((128, 128), jnp.float32)
    for i in range(8):
        c_tmp[8 * i:8 * i + 8, 0:LEV] = c1_ref[0, i]
        c_tmp[64 + 8 * i:72 + 8 * i, 0:LEV] = c2_ref[0, i]
    turned = c_tmp[...].T
    c_send[...] = turned[0:24]
    c_send[18:19, :] = jnp.full((1, 128), flip_i, jnp.int32).astype(jnp.float32)
    c_send[19:20, :] = jnp.full((1, 128), flip_j, jnp.int32).astype(jnp.float32)

    x_load.wait()
    turn = jnp.full((8, 128), flip_j, jnp.int32) == 1

    def pack(n, carry):
        levels = [2 * n, 2 * n + 1]
        for lev in levels:
            for i in range(8):
                fb[SUBSTEPS - 1, lev, pl.ds(i, 8, stride=8), :] = x_vmem[i + flip_i * (7 - 2 * i), lev]
        for lev in levels:
            rows = [fb[SUBSTEPS - 1, lev, 8 * j:8 * j + 8, :] for j in range(8)]
            rows = [jnp.where(turn, rows[7 - j], rows[j]) for j in range(8)]
            for d, v in enumerate(pick_blocks(turn_blocks(rows))):
                send[d, lev] = v
        return carry

    lax.fori_loop(0, LEV // 2, pack, 0)

    pl.semaphore_wait(barrier, len(greeted))

    def block_of(zz, xx):
        return div(rem(zz + 6, 8), 4) * 4 + xx

    def ring_copy(o, sending):
        dz, dx = (2, 6)[o // 4], o % 4
        if sending:
            return rem(z + dz, 8), rem(x + dx, 4), ring
        zs, xs = rem(z + 8 - dz, 8), rem(x + 4 - dx, 4)
        return zs, xs, div(zs, 4) * 4 + xs

    def c_copy(o, sending=True):
        zz, xx, slot = ring_copy(o, sending)
        return pltpu.make_async_remote_copy(
            src_ref=c_send, dst_ref=c_recv.at[pl.ds(slot * 24, 24)],
            send_sem=c_ssem.at[o], recv_sem=c_rsem.at[o], device_id=at(zz, xx), device_id_type=MESH)

    def a_copy(o, ch, sending=True):
        first, count = CHUNKS[ch]
        zz, xx, slot = ring_copy(o, sending)
        return pltpu.make_async_remote_copy(
            src_ref=send.at[block_of(zz, xx), pl.ds(first, count)], dst_ref=recv.at[slot, pl.ds(first, count)],
            send_sem=a_ssem.at[o, ch], recv_sem=a_rsem.at[o, ch], device_id=at(zz, xx), device_id_type=MESH)

    order = [0, 4, 1, 5, 2, 6, 3, 7]
    for o in order:
        begin(("c", o), c_copy(o).start, c_copy(o).wait_send, c_copy(o, False).wait_recv)
    def exchange(ch):
        for o in order:
            begin(("a", ch, o), a_copy(o, ch).start, a_copy(o, ch).wait_send, a_copy(o, ch, False).wait_recv)

    exchange(0)
    w_load.wait()
    diagonal = jnp.where(
        lax.broadcasted_iota(jnp.int32, (72, 72), 0) == lax.broadcasted_iota(jnp.int32, (72, 72), 1), 0.6, 0.0)

    def prepare(cell, carry):
        s, j = cell // 8, cell % 8
        w = w_vmem[s, j]
        total = jnp.sum(w, axis=-1, keepdims=True)
        matrix[cell] = 0.4 * (w / total) + diagonal
        return carry

    lax.fori_loop(0, 16, prepare, 0)
    left(*(("a", 0, o) for o in range(8)))
    exchange(1)

    arrive(*(("c", o) for o in range(8)))
    spread = (
        lax.broadcasted_iota(jnp.int32, (24, 128), 0) % 8 == lax.broadcasted_iota(jnp.int32, (24, 128), 1) // 16
    ).astype(jnp.float32).astype(jnp.bfloat16)

    def spread_level(lev):
        v = c_recv[pl.ds(lev, 8, stride=24), :]
        p0 = v.astype(jnp.bfloat16).astype(jnp.float32)
        p1 = (v - p0).astype(jnp.bfloat16).astype(jnp.float32)
        p2 = v - p0 - p1
        parts = jnp.concatenate([p0, p1, p2], axis=0).astype(jnp.bfloat16)
        return lax.dot_general(parts, spread, (((0,), (0,)), ((), ())), preferred_element_type=jnp.float32)

    def courant(n, carry):
        levels = [3 * n + u for u in range(3)]
        for u, lev in enumerate(levels):
            wide = spread_level(lev)
            for i in range(8):
                for n, value in enumerate(coefficients(wide[8 * i:8 * i + 8])):
                    k1[n, lev, 8 * i + 8:8 * i + 16, :] = value
                    if i == 7:
                        k1[n, lev, 0:8, :] = pltpu.roll(value, 16, 1)
                raw[u, pl.ds(i, 8, stride=8), :] = wide[64 + 8 * i:72 + 8 * i]
        for u, lev in enumerate(levels):
            for j in range(8):
                for n, value in enumerate(coefficients(raw[u, 8 * j:8 * j + 8, :])):
                    k2[n, lev, 8 * j + 8:8 * j + 16, :] = value
            edge_send[lev] = raw[u, 56:64, :]
        return carry

    lax.fori_loop(0, LEV // 3, courant, 0)
    for n in range(2):
        flags[n] = spread_level(18 + n)[0:8]

    edge = pltpu.make_async_remote_copy(
        src_ref=edge_send, dst_ref=edge_recv, send_sem=e_ssem, recv_sem=e_rsem, device_id=high, device_id_type=MESH)
    left(*(("a", 1, o) for o in range(8)))
    exchange(2)
    begin("edge", edge.start, edge.wait_send, edge.wait_recv)

    roll_low = jnp.where(yc == 0, 16, 0)
    roll_high = jnp.where(yc == 7, 112, 0)
    arrival_turn = [16 * rem(slot + 8 - eighth, 8) for slot in range(8)]
    column_turn = [16 * rem(slot + 8 - ring, 8) for slot in range(8)]

    def unpack(ch):
        first, count = CHUNKS[ch]
        arrive(*(("a", ch, o) for o in range(8)))

        def some(n, carry):
            levels = [first + 2 * n, first + 2 * n + 1]
            for lev in levels:
                rows = pick_blocks([pltpu.roll(recv[slot, lev], arrival_turn[slot], 1) for slot in range(8)])
                for j, v in enumerate(turn_back(rows)):
                    fa[lev, pl.ds(j, 8, stride=8), :] = v
            return carry

        lax.fori_loop(0, count // 2, some, 0)

    def advance(q, low_cells, high_cells, k, lev):
        e = low_cells + q + high_cells
        a = [face_value(*e[n:n + 4]) for n in range(11)]
        flux = [
            face_flux(a[f + 1], a[f], a[f + 2], e[f + 2], e[f + 3], *(k[n, lev, 8 * f:8 * f + 8, :] for n in range(3)))
            for f in range(9)]
        return [q[n] - (flux[n + 1] - flux[n]) for n in range(8)]

    def sweep_first(step, ch):
        first, count = CHUNKS[ch]

        def level(lev):
            q = [fa[lev, 8 * i:8 * i + 8, :] for i in range(8)]
            return advance(q, [pltpu.roll(v, 16, 1) for v in q[5:]], [pltpu.roll(v, 112, 1) for v in q[:3]], k1, lev)

        def some(n, carry):
            levels = [first + n * UNROLL + k for k in range(UNROLL)]
            new = [level(lev) for lev in levels]
            for lev, rows in zip(levels, new):
                for i in range(8):
                    fb[step, lev, pl.ds(i, 8, stride=8), :] = rows[i]
            return carry

        lax.fori_loop(0, count // UNROLL, some, 0)

    def halo_copies(step, ch):
        first, count = CHUNKS[ch]
        return (
            pltpu.make_async_remote_copy(
                src_ref=fb.at[step, pl.ds(first, count), pl.ds(40, 24)], dst_ref=halo_low.at[step, pl.ds(first, count)],
                send_sem=h_ssem.at[0, step, ch], recv_sem=h_rsem.at[0, step, ch], device_id=high, device_id_type=MESH),
            pltpu.make_async_remote_copy(
                src_ref=fb.at[step, pl.ds(first, count), pl.ds(0, 24)], dst_ref=halo_high.at[step, pl.ds(first, count)],
                send_sem=h_ssem.at[1, step, ch], recv_sem=h_rsem.at[1, step, ch], device_id=low, device_id_type=MESH),
        )

    def sweep_second(step, ch):
        first, count = CHUNKS[ch]
        last = step == SUBSTEPS - 1

        def level(lev):
            q = [fb[step, lev, 8 * j:8 * j + 8, :] for j in range(8)]
            new = advance(
                q, [pltpu.roll(halo_low[step, lev, 8 * j:8 * j + 8, :], roll_low, 1) for j in range(3)],
                [pltpu.roll(halo_high[step, lev, 8 * j:8 * j + 8, :], roll_high, 1) for j in range(3)], k2, lev)
            if last:
                back = flags[1] > 0.5
                new = [jnp.where(back, new[7 - j], new[j]) for j in range(8)]
            return new

        def some(n, carry):
            levels = [first + n * UNROLL + k for k in range(UNROLL)]
            new = [level(lev) for lev in levels]
            for lev, rows in zip(levels, new):
                for j in range(8):
                    fa[lev, pl.ds(j, 8, stride=8), :] = rows[j]
            return carry

        lax.fori_loop(0, count // UNROLL, some, 0)

    def edge_levels(n, carry):
        for lev in [6 * n + u for u in range(6)]:
            for n, value in enumerate(coefficients(pltpu.roll(edge_recv[lev], roll_low, 1))):
                k2[n, lev, 0:8, :] = value
        return carry

    def mix_pack(ch):
        groups = GROUPS[ch]

        def one(r, carry):
            back = flags[0] > 0.5
            for m in groups:
                rows = []
                for k in range(8):
                    lev, i = 4 * m + k // 2, 2 * r + k % 2
                    if lev < LEV:
                        here = fa[lev, pl.ds(pl.multiple_of(8 * i, 8), 8), :]
                        there = fa[lev, pl.ds(pl.multiple_of(56 - 8 * i, 8), 8), :]
                        rows.append(jnp.where(back, there, here))
                    else:
                        rows.append(jnp.zeros((8, 128), jnp.float32))
                for k, v in enumerate(pick_blocks(turn_blocks(rows))):
                    mix_send[k * 4 + r, m] = v
            return carry

        lax.fori_loop(0, 4, one, 0)

    def m_copy(o, ch):
        zd, xd = rem(z + div(o, 4), 8), rem(x + rem(o, 4), 4)
        part = pl.ds(GROUPS[ch][0], len(GROUPS[ch]))
        return pltpu.make_async_remote_copy(
            src_ref=mix_send.at[(div(zd, 4) * 4 + xd) * 4 + rem(zd, 4), part], dst_ref=mix_recv.at[group * 8 + eighth, part],
            send_sem=m_ssem.at[ch, o], recv_sem=m_rsem.at[ch, o], device_id=at(zd, xd), device_id_type=MESH)

    def m_arrival(o, ch):
        zs, xs = rem(z + 8 - div(o, 4), 8), rem(x + 4 - rem(o, 4), 4)
        slot = rem(zs + 2, 4) * 8 + block_of(zs, xs)
        part = pl.ds(GROUPS[ch][0], len(GROUPS[ch]))
        return pltpu.make_async_remote_copy(
            src_ref=mix_send.at[0, part], dst_ref=mix_recv.at[slot, part],
            send_sem=m_ssem.at[ch, o], recv_sem=m_rsem.at[ch, o], device_id=at(zs, xs), device_id_type=MESH)

    own = [
        pltpu.make_async_copy(
            mix_send.at[ring * 4 + l, pl.ds(groups[0], len(groups))],
            mix_recv.at[group * 8 + eighth, pl.ds(groups[0], len(groups))], l_sem.at[2 + ch])
        for ch, groups in enumerate(GROUPS)
    ]

    def segment(step, ch):
        if step == 0:
            unpack(ch)
        else:
            arrive(("h", step - 1, ch, 0), ("h", step - 1, ch, 1))
            sweep_second(step - 1, ch)
        if step < SUBSTEPS:
            sweep_first(step, ch)
            for side, copy in enumerate(halo_copies(step, ch)):
                begin(("h", step, ch, side), copy.start, copy.wait_send, copy.wait_recv)
            return
        mix_pack(ch)

        def others(action):
            def run():
                def one(o, carry):
                    action(o)
                    return carry

                lax.fori_loop(1, 32, one, 0)

            return run

        begin(
            ("m", ch), others(lambda o: m_copy(o, ch).start()),
            others(lambda o: m_copy(o, ch).wait_send()), others(lambda o: m_arrival(o, ch).wait_recv()))
        begin(("own", ch), own[ch].start, lambda: None, own[ch].wait)

    for wave in range(SUBSTEPS + NCH):
        if wave == 1:
            arrive("edge")
            lax.fori_loop(0, LEV // 6, edge_levels, 0)
        for ch in range(NCH):
            if 0 <= wave - ch <= SUBSTEPS:
                segment(wave - ch, ch)

    for ch in range(NCH):
        arrive(("m", ch), ("own", ch))

    def mix_unpack(g, carry):
        for m in range(5):
            rows = pick_blocks([pltpu.roll(mix_recv[g * 8 + k, m], column_turn[k], 1) for k in range(8)])
            rows = turn_back(rows)
            for k in range(8):
                lev, s = 4 * m + k // 2, k % 2
                if lev < LEV:
                    columns[s, pl.ds(pl.multiple_of((g * LEV + lev) * 8, 8), 8), :] = rows[k]
        return carry

    lax.fori_loop(0, 4, mix_unpack, 0)

    def d_copy(s, o):
        to = rem(l + o, 4)
        return pltpu.make_async_remote_copy(
            src_ref=mixed.at[s, pl.ds(to * 144, 144)], dst_ref=o_ref.at[0, 2 * l + s],
            send_sem=d_ssem.at[s, o], recv_sem=d_rsem.at[s, o], device_id={"tile": t, "lev": to}, device_id_type=MESH)

    def d_arrival(s, o):
        source = rem(l + 4 - o, 4)
        return pltpu.make_async_remote_copy(
            src_ref=mixed.at[s, pl.ds(0, 144)], dst_ref=o_ref.at[0, 2 * source + s],
            send_sem=d_ssem.at[s, o], recv_sem=d_rsem.at[s, o], device_id={"tile": t, "lev": source}, device_id_type=MESH)

    def mix_row(s):
        def one(j, carry):
            v = columns[s, pl.ds(j, 72, stride=8), :]
            v_hi = v.astype(jnp.bfloat16)
            v_lo = (v - v_hi.astype(jnp.float32)).astype(jnp.bfloat16)
            m = matrix[s * 8 + j]
            m_hi = m.astype(jnp.bfloat16)
            m_lo = (m - m_hi.astype(jnp.float32)).astype(jnp.bfloat16)
            dot = lambda a, b: jnp.dot(a, b, preferred_element_type=jnp.float32)
            out = dot(m_hi, v_hi) + (dot(m_hi, v_lo) + dot(m_lo, v_hi))
            mixed[s, pl.ds(j, 72, stride=8), :] = out
            return carry

        lax.fori_loop(0, 8, one, 0)

    for s in range(2):
        mix_row(s)
        for o in range(1, 4):
            begin(("d", s, o), d_copy(s, o).start, d_copy(s, o).wait_send, d_arrival(s, o).wait_recv)
        local = pltpu.make_async_copy(mixed.at[s, pl.ds(l * 144, 144)], o_ref.at[0, 2 * l + s], l_sem.at[s])
        begin(("local", s), local.start, lambda: None, local.wait)

    for arrived, sent in pending.values():
        if arrived is not None:
            arrived()
        sent()


def solution(mesh):
    f32 = jnp.float32

    def on_device(tracers, courant_first, courant_second, weights, frame_flip):
        vmem = pl.BlockSpec(memory_space=pltpu.VMEM)
        hbm = pl.BlockSpec(memory_space=pl.ANY)
        dma = pltpu.SemaphoreType.DMA
        rows = jnp.transpose(tracers, (0, 1, 3, 2, 4)).reshape(1, 8, LEV, 8, 128)
        out = pl.pallas_call(
            kernel,
            out_shape=jax.ShapeDtypeStruct((1, 8, LEV * 8, 128), f32),
            in_specs=[hbm, vmem, vmem, hbm, pl.BlockSpec(memory_space=pltpu.SMEM)],
            out_specs=vmem,
            scratch_shapes=[
                pltpu.VMEM((8, LEV, 8, 128), f32),
                pltpu.VMEM((2, 8, 72, 72), f32),
                pltpu.VMEM((8, LEV, 8, 128), f32),
                pltpu.VMEM((8, LEV, 8, 128), f32),
                pltpu.VMEM((128, 128), f32),
                pltpu.VMEM((24, 128), f32),
                pltpu.VMEM((192, 128), f32),
                pltpu.VMEM((3, 64, 128), f32),
                pltpu.VMEM((2, 8, 128), f32),
                pltpu.VMEM((LEV, 64, 128), f32),
                pltpu.VMEM((SUBSTEPS, LEV, 64, 128), f32),
                pltpu.VMEM((SUBSTEPS, LEV, 24, 128), f32),
                pltpu.VMEM((SUBSTEPS, LEV, 24, 128), f32),
                pltpu.VMEM((LEV, 8, 128), f32),
                pltpu.VMEM((LEV, 8, 128), f32),
                pltpu.VMEM((3, LEV, 72, 128), f32),
                pltpu.VMEM((3, LEV, 72, 128), f32),
                pltpu.VMEM((32, 5, 8, 128), f32),
                pltpu.VMEM((32, 5, 8, 128), f32),
                pltpu.VMEM((2, 72 * 8, 128), f32),
                pltpu.VMEM((16, 72, 72), f32),
                pltpu.VMEM((2, 72 * 8, 128), f32),
                dma((8, NCH)), dma((8, NCH)),
                dma((8,)), dma((8,)),
                dma((2, SUBSTEPS, NCH)), dma((2, SUBSTEPS, NCH)),
                dma, dma,
                dma((NCH, 32)), dma((NCH, 32)),
                dma((2, 4)), dma((2, 4)),
                dma((2 + NCH,)),
                dma((2,)),
            ],
            compiler_params=pltpu.CompilerParams(collective_id=0, has_side_effects=True),
        )(rows, courant_first, courant_second, weights, frame_flip)
        return jnp.transpose(out.reshape(1, 8, LEV, 8, 128), (0, 1, 3, 2, 4))

    return jax.shard_map(
        on_device,
        mesh=mesh,
        in_specs=(
            P("tile", None, None, "lev", None),
            P("tile", None, None, "lev"),
            P("tile", None, None, "lev"),
            P("tile", "lev", None, None, None),
            P("tile", None),
        ),
        out_specs=P("tile", None, None, "lev", None),
        check_vma=False,
    )
```

```python
import functools

import jax
import jax.numpy as jnp
from jax import lax
from jax.experimental import pallas as pl
from jax.experimental.pallas import tpu as pltpu
from jax.sharding import PartitionSpec as P

MESH = pl.DeviceIdType.MESH
SUBSTEPS = 3
LEV = 18
CHUNKS = ((0, 8), (8, 4), (12, 6))
NCH = len(CHUNKS)
SCHEDULE = (
    ("courant", 0), ("send", 1), ("step", 0, 0), ("courant", 1), ("send", 2), ("step", 1, 0), ("step", 0, 1),
    ("courant", 2), ("flags", 0), ("step", 1, 1), ("step", 0, 2), ("step", 2, 0), ("step", 1, 2), ("step", 0, 3),
    ("scatter", 0), ("step", 2, 1), ("step", 1, 3), ("scatter", 1), ("step", 2, 2), ("step", 2, 3), ("scatter", 2),
)
GROUPS = tuple(tuple(range(first // 4, (first + count + 3) // 4)) for first, count in CHUNKS)
UNROLL = 2


def turn_blocks(rows):
    return [pltpu.roll(v, 16 * k, 1) if k else v for k, v in enumerate(rows)]


def pick_blocks(rows):
    block = lax.broadcasted_iota(jnp.int32, (8, 128), 1) // 16
    rows = [rows[(8 - b) % 8] for b in range(8)]
    for m in (1, 2, 4):
        other = (block & m) != 0
        rows = [jnp.where(other, rows[(b + 8 - m) % 8], rows[b]) for b in range(8)]
    return rows


def turn_back(rows):
    return [pltpu.roll(v, 128 - 16 * b, 1) if b else v for b, v in enumerate(rows)]


def coefficients(c):
    up = c >= 0.0
    half = 0.5 * c * c
    b = half * (1.0 - jnp.abs(c) * (2.0 / 3.0))
    b = jnp.where(up, b, -b)
    signed = jnp.where(up, half, -half)
    return (c - signed - 3.0 * b) * (1.0 / 12.0), (signed - 3.0 * b) * (1.0 / 12.0), 6.0 * b


def face_value(q0, q1, q2, q3):
    return 7.0 * (q1 + q2) - (q0 + q3)


def face_flux(mid, below, above, q_below, q_above, ka, ku, kq):
    up = kq >= 0.0
    return ka * mid + ku * jnp.where(up, below, above) + kq * jnp.where(up, q_below, q_above)


def kernel(
    x_ref, c1_ref, c2_ref, w_ref, f_ref, o_ref,
    x_vmem, w_vmem, send, recv, c_tmp, c_send, c_recv, raw, flags,
    fa, fb, halo_low, halo_high, edge_send, edge_recv,
    k1, k2, mix_send, mix_recv, columns, matrix, mixed,
    a_ssem, a_rsem, c_ssem, c_rsem, h_ssem, h_rsem, e_ssem, e_rsem, m_ssem, m_rsem, d_ssem, d_rsem, l_sem, i_sem,
):
    t = lax.axis_index("tile")
    l = lax.axis_index("lev")
    div, rem = lax.div, lax.rem
    ring = div(t, 8)
    yc = rem(t, 8)
    hi = div(ring, 4)
    x = rem(ring, 4)
    z = hi * 4 + l
    group = rem(l + 2, 4)
    eighth = div(rem(z + 6, 8), 4) * 4 + x

    def at(zz, xx):
        return {"tile": (div(zz, 4) * 4 + xx) * 8 + yc, "lev": rem(zz, 4)}

    low = {"tile": ring * 8 + rem(yc + 7, 8), "lev": l}
    high = {"tile": ring * 8 + rem(yc + 1, 8), "lev": l}

    pending = {}

    def begin(key, start, sent, arrived):
        start()
        pending[key] = [arrived, sent]

    def left(*keys):
        for key in keys:
            pending[key][1]()
            pending[key][1] = lambda: None

    def arrive(*keys):
        for key in keys:
            pending[key][0]()
            pending[key][0] = None

    barrier = pltpu.get_barrier_semaphore()
    greeted = [at(rem(z + dz, 8), rem(x + dx, 4)) for dz in (2, 6) for dx in range(4)]
    greeted += [at(rem(z + 1, 8), x), at(rem(z + 7, 8), x), low, high]
    for device in greeted:
        pl.semaphore_signal(barrier, inc=1, device_id=device, device_id_type=MESH)
    x_load = pltpu.make_async_copy(x_ref.at[0], x_vmem, i_sem.at[0])
    w_load = pltpu.make_async_copy(w_ref.at[0], w_vmem, i_sem.at[1])
    x_load.start()
    w_load.start()

    flip_i = f_ref[0, 0]
    flip_j = f_ref[0, 1]
    c_tmp[...] = jnp.zeros((128, 128), jnp.float32)
    for i in range(8):
        c_tmp[8 * i:8 * i + 8, 0:LEV] = c1_ref[0, i]
        c_tmp[64 + 8 * i:72 + 8 * i, 0:LEV] = c2_ref[0, i]
    turned = c_tmp[...].T
    c_send[...] = turned[0:24]
    c_send[18:19, :] = jnp.full((1, 128), flip_i, jnp.int32).astype(jnp.float32)
    c_send[19:20, :] = jnp.full((1, 128), flip_j, jnp.int32).astype(jnp.float32)

    x_load.wait()
    turn = jnp.full((8, 128), flip_j, jnp.int32) == 1

    def pack(n, carry):
        levels = [2 * n, 2 * n + 1]
        for lev in levels:
            for i in range(8):
                fb[SUBSTEPS - 1, lev, pl.ds(i, 8, stride=8), :] = x_vmem[i + flip_i * (7 - 2 * i), lev]
        for lev in levels:
            rows = [fb[SUBSTEPS - 1, lev, 8 * j:8 * j + 8, :] for j in range(8)]
            rows = [jnp.where(turn, rows[7 - j], rows[j]) for j in range(8)]
            for d, v in enumerate(pick_blocks(turn_blocks(rows))):
                send[d, lev] = v
        return carry

    lax.fori_loop(0, LEV // 2, pack, 0)

    pl.semaphore_wait(barrier, len(greeted))

    def block_of(zz, xx):
        return div(rem(zz + 6, 8), 4) * 4 + xx

    def ring_copy(o, sending):
        dz, dx = (2, 6)[o // 4], o % 4
        if sending:
            return rem(z + dz, 8), rem(x + dx, 4), ring
        zs, xs = rem(z + 8 - dz, 8), rem(x + 4 - dx, 4)
        return zs, xs, div(zs, 4) * 4 + xs

    def c_copy(o, sending=True):
        zz, xx, slot = ring_copy(o, sending)
        return pltpu.make_async_remote_copy(
            src_ref=c_send, dst_ref=c_recv.at[pl.ds(slot * 24, 24)],
            send_sem=c_ssem.at[o], recv_sem=c_rsem.at[o], device_id=at(zz, xx), device_id_type=MESH)

    def a_copy(o, ch, sending=True):
        first, count = CHUNKS[ch]
        zz, xx, slot = ring_copy(o, sending)
        return pltpu.make_async_remote_copy(
            src_ref=send.at[block_of(zz, xx), pl.ds(first, count)], dst_ref=recv.at[slot, pl.ds(first, count)],
            send_sem=a_ssem.at[o, ch], recv_sem=a_rsem.at[o, ch], device_id=at(zz, xx), device_id_type=MESH)

    order = [0, 4, 1, 5, 2, 6, 3, 7]
    for o in order:
        begin(("c", o), c_copy(o).start, c_copy(o).wait_send, c_copy(o, False).wait_recv)
    def exchange(ch):
        for o in order:
            begin(("a", ch, o), a_copy(o, ch).start, a_copy(o, ch).wait_send, a_copy(o, ch, False).wait_recv)

    exchange(0)
    w_load.wait()
    diagonal = jnp.where(
        lax.broadcasted_iota(jnp.int32, (72, 72), 0) == lax.broadcasted_iota(jnp.int32, (72, 72), 1), 0.6, 0.0)

    def prepare(cell, carry):
        s, j = cell // 8, cell % 8
        w = w_vmem[s, j]
        total = jnp.sum(w, axis=-1, keepdims=True)
        matrix[cell] = 0.4 * (w / total) + diagonal
        return carry

    lax.fori_loop(0, 16, prepare, 0)

    arrive(*(("c", o) for o in range(8)))
    spread = (
        lax.broadcasted_iota(jnp.int32, (24, 128), 0) % 8 == lax.broadcasted_iota(jnp.int32, (24, 128), 1) // 16
    ).astype(jnp.float32).astype(jnp.bfloat16)

    def spread_level(lev):
        v = c_recv[pl.ds(lev, 8, stride=24), :]
        p0 = v.astype(jnp.bfloat16).astype(jnp.float32)
        p1 = (v - p0).astype(jnp.bfloat16).astype(jnp.float32)
        p2 = v - p0 - p1
        parts = jnp.concatenate([p0, p1, p2], axis=0).astype(jnp.bfloat16)
        return lax.dot_general(parts, spread, (((0,), (0,)), ((), ())), preferred_element_type=jnp.float32)

    def courant(first, width, n, carry):
        levels = [first + width * n + u for u in range(width)]
        for u, lev in enumerate(levels):
            wide = spread_level(lev)
            for i in range(8):
                for n, value in enumerate(coefficients(wide[8 * i:8 * i + 8])):
                    k1[n, lev, 8 * i + 8:8 * i + 16, :] = value
                    if i == 7:
                        k1[n, lev, 0:8, :] = pltpu.roll(value, 16, 1)
                raw[u, pl.ds(i, 8, stride=8), :] = wide[64 + 8 * i:72 + 8 * i]
        for u, lev in enumerate(levels):
            for j in range(8):
                for n, value in enumerate(coefficients(raw[u, 8 * j:8 * j + 8, :])):
                    k2[n, lev, 8 * j + 8:8 * j + 16, :] = value
            edge_send[lev] = raw[u, 56:64, :]
        return carry

    def edge_copy(ch):
        part = pl.ds(*CHUNKS[ch])
        return pltpu.make_async_remote_copy(
            src_ref=edge_send.at[part], dst_ref=edge_recv.at[part],
            send_sem=e_ssem.at[ch], recv_sem=e_rsem.at[ch], device_id=high, device_id_type=MESH)

    def courant_chunk(ch):
        first, count = CHUNKS[ch]
        width = 3 if count % 3 == 0 else 2
        lax.fori_loop(0, count // width, functools.partial(courant, first, width), 0)
        edge = edge_copy(ch)
        begin(("e", ch), edge.start, edge.wait_send, edge.wait_recv)

    roll_low = jnp.where(yc == 0, 16, 0)
    roll_high = jnp.where(yc == 7, 112, 0)
    arrival_turn = [16 * rem(slot + 8 - eighth, 8) for slot in range(8)]
    column_turn = [16 * rem(slot + 8 - ring, 8) for slot in range(8)]

    def unpack(ch):
        first, count = CHUNKS[ch]
        arrive(*(("a", ch, o) for o in range(8)))

        def some(n, carry):
            levels = [first + 2 * n, first + 2 * n + 1]
            for lev in levels:
                rows = pick_blocks([pltpu.roll(recv[slot, lev], arrival_turn[slot], 1) for slot in range(8)])
                for j, v in enumerate(turn_back(rows)):
                    fa[lev, pl.ds(j, 8, stride=8), :] = v
            return carry

        lax.fori_loop(0, count // 2, some, 0)

    def advance(q, low_cells, high_cells, k, lev):
        e = low_cells + q + high_cells
        a = [face_value(*e[n:n + 4]) for n in range(11)]
        flux = [
            face_flux(a[f + 1], a[f], a[f + 2], e[f + 2], e[f + 3], *(k[n, lev, 8 * f:8 * f + 8, :] for n in range(3)))
            for f in range(9)]
        return [q[n] - (flux[n + 1] - flux[n]) for n in range(8)]

    def sweep_first(step, ch):
        first, count = CHUNKS[ch]

        def level(lev):
            q = [fa[lev, 8 * i:8 * i + 8, :] for i in range(8)]
            return advance(q, [pltpu.roll(v, 16, 1) for v in q[5:]], [pltpu.roll(v, 112, 1) for v in q[:3]], k1, lev)

        def some(n, carry):
            levels = [first + n * UNROLL + k for k in range(UNROLL)]
            new = [level(lev) for lev in levels]
            for lev, rows in zip(levels, new):
                for i in range(8):
                    fb[step, lev, pl.ds(i, 8, stride=8), :] = rows[i]
            return carry

        lax.fori_loop(0, count // UNROLL, some, 0)

    def halo_copies(step, ch):
        first, count = CHUNKS[ch]
        return (
            pltpu.make_async_remote_copy(
                src_ref=fb.at[step, pl.ds(first, count), pl.ds(40, 24)], dst_ref=halo_low.at[step, pl.ds(first, count)],
                send_sem=h_ssem.at[0, step, ch], recv_sem=h_rsem.at[0, step, ch], device_id=high, device_id_type=MESH),
            pltpu.make_async_remote_copy(
                src_ref=fb.at[step, pl.ds(first, count), pl.ds(0, 24)], dst_ref=halo_high.at[step, pl.ds(first, count)],
                send_sem=h_ssem.at[1, step, ch], recv_sem=h_rsem.at[1, step, ch], device_id=low, device_id_type=MESH),
        )

    def sweep_second(step, ch):
        first, count = CHUNKS[ch]
        last = step == SUBSTEPS - 1

        def level(lev):
            q = [fb[step, lev, 8 * j:8 * j + 8, :] for j in range(8)]
            new = advance(
                q, [pltpu.roll(halo_low[step, lev, 8 * j:8 * j + 8, :], roll_low, 1) for j in range(3)],
                [pltpu.roll(halo_high[step, lev, 8 * j:8 * j + 8, :], roll_high, 1) for j in range(3)], k2, lev)
            if last:
                back = flags[1] > 0.5
                new = [jnp.where(back, new[7 - j], new[j]) for j in range(8)]
            return new

        def some(n, carry):
            levels = [first + n * UNROLL + k for k in range(UNROLL)]
            new = [level(lev) for lev in levels]
            for lev, rows in zip(levels, new):
                for j in range(8):
                    fa[lev, pl.ds(j, 8, stride=8), :] = rows[j]
            return carry

        lax.fori_loop(0, count // UNROLL, some, 0)

    def edge_chunk(ch):
        first, count = CHUNKS[ch]
        arrive(("e", ch))

        def some(n, carry):
            for lev in [first + 2 * n, first + 2 * n + 1]:
                for n, value in enumerate(coefficients(pltpu.roll(edge_recv[lev], roll_low, 1))):
                    k2[n, lev, 0:8, :] = value
            return carry

        lax.fori_loop(0, count // 2, some, 0)

    def mix_pack(ch):
        groups = GROUPS[ch]

        def one(r, carry):
            back = flags[0] > 0.5
            for m in groups:
                rows = []
                for k in range(8):
                    lev, i = 4 * m + k // 2, 2 * r + k % 2
                    if lev < LEV:
                        here = fa[lev, pl.ds(pl.multiple_of(8 * i, 8), 8), :]
                        there = fa[lev, pl.ds(pl.multiple_of(56 - 8 * i, 8), 8), :]
                        rows.append(jnp.where(back, there, here))
                    else:
                        rows.append(jnp.zeros((8, 128), jnp.float32))
                for k, v in enumerate(pick_blocks(turn_blocks(rows))):
                    mix_send[k * 4 + r, m] = v
            return carry

        lax.fori_loop(0, 4, one, 0)

    def m_copy(o, ch):
        dz, dx = (o // 4, o % 4) if isinstance(o, int) else (div(o, 4), rem(o, 4))
        zd, xd = rem(z + dz, 8), rem(x + dx, 4)
        part = pl.ds(GROUPS[ch][0], len(GROUPS[ch]))
        return pltpu.make_async_remote_copy(
            src_ref=mix_send.at[(div(zd, 4) * 4 + xd) * 4 + rem(zd, 4), part], dst_ref=mix_recv.at[group * 8 + eighth, part],
            send_sem=m_ssem.at[ch, o], recv_sem=m_rsem.at[ch, o], device_id=at(zd, xd), device_id_type=MESH)

    def m_arrival(o, ch):
        zs, xs = rem(z + 8 - div(o, 4), 8), rem(x + 4 - rem(o, 4), 4)
        slot = rem(zs + 2, 4) * 8 + block_of(zs, xs)
        part = pl.ds(GROUPS[ch][0], len(GROUPS[ch]))
        return pltpu.make_async_remote_copy(
            src_ref=mix_send.at[0, part], dst_ref=mix_recv.at[slot, part],
            send_sem=m_ssem.at[ch, o], recv_sem=m_rsem.at[ch, o], device_id=at(zs, xs), device_id_type=MESH)

    own = [
        pltpu.make_async_copy(
            mix_send.at[ring * 4 + l, pl.ds(groups[0], len(groups))],
            mix_recv.at[group * 8 + eighth, pl.ds(groups[0], len(groups))], l_sem.at[2 + ch])
        for ch, groups in enumerate(GROUPS)
    ]

    def segment(step, ch):
        if step == 0:
            unpack(ch)
        else:
            if step == 1:
                edge_chunk(ch)
            arrive(("h", step - 1, ch, 0), ("h", step - 1, ch, 1))
            sweep_second(step - 1, ch)
        if step < SUBSTEPS:
            sweep_first(step, ch)
            for side, copy in enumerate(halo_copies(step, ch)):
                begin(("h", step, ch, side), copy.start, copy.wait_send, copy.wait_recv)

    def others(action):
        def run():
            def one(o, carry):
                action(o)
                return carry

            lax.fori_loop(1, 32, one, 0)

        return run

    def scatter(ch):
        mix_pack(ch)

        def far_first():
            for dz in (4, 3, 5, 2, 6, 1, 7, 0):
                for dx in (2, 1, 3, 0):
                    if dz or dx:
                        m_copy(4 * dz + dx, ch).start()

        begin(
            ("m", ch), far_first,
            others(lambda o: m_copy(o, ch).wait_send()), others(lambda o: m_arrival(o, ch).wait_recv()))
        begin(("own", ch), own[ch].start, lambda: None, own[ch].wait)

    for what, ch, *step in SCHEDULE:
        if what == "send":
            left(*(("a", ch - 1, o) for o in range(8)))
            exchange(ch)
        elif what == "flags":
            for n in range(2):
                flags[n] = spread_level(LEV + n)[0:8]
        elif what == "courant":
            courant_chunk(ch)
        elif what == "scatter":
            scatter(ch)
        else:
            segment(step[0], ch)

    for ch in range(NCH):
        arrive(("m", ch), ("own", ch))

    def mix_unpack(g, carry):
        for m in range(5):
            rows = pick_blocks([pltpu.roll(mix_recv[g * 8 + k, m], column_turn[k], 1) for k in range(8)])
            rows = turn_back(rows)
            for k in range(8):
                lev, s = 4 * m + k // 2, k % 2
                if lev < LEV:
                    columns[s, pl.ds(pl.multiple_of((g * LEV + lev) * 8, 8), 8), :] = rows[k]
        return carry

    lax.fori_loop(0, 4, mix_unpack, 0)

    def d_copy(s, o):
        to = rem(l + o, 4)
        return pltpu.make_async_remote_copy(
            src_ref=mixed.at[s, pl.ds(to * 144, 144)], dst_ref=o_ref.at[0, 2 * l + s],
            send_sem=d_ssem.at[s, o], recv_sem=d_rsem.at[s, o], device_id={"tile": t, "lev": to}, device_id_type=MESH)

    def d_arrival(s, o):
        source = rem(l + 4 - o, 4)
        return pltpu.make_async_remote_copy(
            src_ref=mixed.at[s, pl.ds(0, 144)], dst_ref=o_ref.at[0, 2 * source + s],
            send_sem=d_ssem.at[s, o], recv_sem=d_rsem.at[s, o], device_id={"tile": t, "lev": source}, device_id_type=MESH)

    def mix_row(s):
        def one(j, carry):
            v = columns[s, pl.ds(j, 72, stride=8), :]
            v_hi = v.astype(jnp.bfloat16)
            v_lo = (v - v_hi.astype(jnp.float32)).astype(jnp.bfloat16)
            m = matrix[s * 8 + j]
            m_hi = m.astype(jnp.bfloat16)
            m_lo = (m - m_hi.astype(jnp.float32)).astype(jnp.bfloat16)
            dot = lambda a, b: jnp.dot(a, b, preferred_element_type=jnp.float32)
            out = dot(m_hi, v_hi) + (dot(m_hi, v_lo) + dot(m_lo, v_hi))
            mixed[s, pl.ds(j, 72, stride=8), :] = out
            return carry

        lax.fori_loop(0, 8, one, 0)

    for s in range(2):
        mix_row(s)
        for o in range(1, 4):
            begin(("d", s, o), d_copy(s, o).start, d_copy(s, o).wait_send, d_arrival(s, o).wait_recv)
        local = pltpu.make_async_copy(mixed.at[s, pl.ds(l * 144, 144)], o_ref.at[0, 2 * l + s], l_sem.at[s])
        begin(("local", s), local.start, lambda: None, local.wait)

    for arrived, sent in pending.values():
        if arrived is not None:
            arrived()
        sent()


def solution(mesh):
    f32 = jnp.float32

    def on_device(tracers, courant_first, courant_second, weights, frame_flip):
        vmem = pl.BlockSpec(memory_space=pltpu.VMEM)
        hbm = pl.BlockSpec(memory_space=pl.ANY)
        dma = pltpu.SemaphoreType.DMA
        rows = jnp.transpose(tracers, (0, 1, 3, 2, 4)).reshape(1, 8, LEV, 8, 128)
        out = pl.pallas_call(
            kernel,
            out_shape=jax.ShapeDtypeStruct((1, 8, LEV * 8, 128), f32),
            in_specs=[hbm, vmem, vmem, hbm, pl.BlockSpec(memory_space=pltpu.SMEM)],
            out_specs=vmem,
            scratch_shapes=[
                pltpu.VMEM((8, LEV, 8, 128), f32),
                pltpu.VMEM((2, 8, 72, 72), f32),
                pltpu.VMEM((8, LEV, 8, 128), f32),
                pltpu.VMEM((8, LEV, 8, 128), f32),
                pltpu.VMEM((128, 128), f32),
                pltpu.VMEM((24, 128), f32),
                pltpu.VMEM((192, 128), f32),
                pltpu.VMEM((3, 64, 128), f32),
                pltpu.VMEM((2, 8, 128), f32),
                pltpu.VMEM((LEV, 64, 128), f32),
                pltpu.VMEM((SUBSTEPS, LEV, 64, 128), f32),
                pltpu.VMEM((SUBSTEPS, LEV, 24, 128), f32),
                pltpu.VMEM((SUBSTEPS, LEV, 24, 128), f32),
                pltpu.VMEM((LEV, 8, 128), f32),
                pltpu.VMEM((LEV, 8, 128), f32),
                pltpu.VMEM((3, LEV, 72, 128), f32),
                pltpu.VMEM((3, LEV, 72, 128), f32),
                pltpu.VMEM((32, 5, 8, 128), f32),
                pltpu.VMEM((32, 5, 8, 128), f32),
                pltpu.VMEM((2, 72 * 8, 128), f32),
                pltpu.VMEM((16, 72, 72), f32),
                pltpu.VMEM((2, 72 * 8, 128), f32),
                dma((8, NCH)), dma((8, NCH)),
                dma((8,)), dma((8,)),
                dma((2, SUBSTEPS, NCH)), dma((2, SUBSTEPS, NCH)),
                dma((NCH,)), dma((NCH,)),
                dma((NCH, 32)), dma((NCH, 32)),
                dma((2, 4)), dma((2, 4)),
                dma((2 + NCH,)),
                dma((2,)),
            ],
            compiler_params=pltpu.CompilerParams(collective_id=0, has_side_effects=True),
        )(rows, courant_first, courant_second, weights, frame_flip)
        return jnp.transpose(out.reshape(1, 8, LEV, 8, 128), (0, 1, 3, 2, 4))

    return jax.shard_map(
        on_device,
        mesh=mesh,
        in_specs=(
            P("tile", None, None, "lev", None),
            P("tile", None, None, "lev"),
            P("tile", None, None, "lev"),
            P("tile", "lev", None, None, None),
            P("tile", None),
        ),
        out_specs=P("tile", None, None, "lev", None),
        check_vma=False,
    )
```

```python
import functools

import jax
import jax.numpy as jnp
from jax import lax
from jax.experimental import pallas as pl
from jax.experimental.pallas import tpu as pltpu
from jax.sharding import PartitionSpec as P

MESH = pl.DeviceIdType.MESH
SUBSTEPS = 3
LEV = 18
CHUNKS = ((0, 8), (8, 4), (12, 6))
NCH = len(CHUNKS)
SCHEDULE = (
    ("courant", 0), ("send", 1), ("step", 0, 0), ("courant", 1), ("send", 2), ("courant", 2), ("flags", 0),
    ("step", 0, 1), ("step", 1, 0), ("step", 0, 2), ("step", 1, 1), ("step", 2, 0), ("step", 0, 3), ("scatter", 0),
    ("step", 1, 2), ("step", 2, 1), ("step", 1, 3), ("scatter", 1), ("step", 2, 2), ("step", 2, 3), ("scatter", 2),
)
GROUPS = tuple(tuple(range(first // 4, (first + count + 3) // 4)) for first, count in CHUNKS)
UNROLL = 2
CELLS = 4


def turn_blocks(rows):
    return [pltpu.roll(v, 16 * k, 1) if k else v for k, v in enumerate(rows)]


def pick_blocks(rows):
    block = lax.broadcasted_iota(jnp.int32, (8, 128), 1) // 16
    rows = [rows[(8 - b) % 8] for b in range(8)]
    for m in (1, 2, 4):
        other = (block & m) != 0
        rows = [jnp.where(other, rows[(b + 8 - m) % 8], rows[b]) for b in range(8)]
    return rows


def turn_back(rows):
    return [pltpu.roll(v, 128 - 16 * b, 1) if b else v for b, v in enumerate(rows)]


def coefficients(c):
    up = c >= 0.0
    half = 0.5 * c * c
    b = half * (1.0 - jnp.abs(c) * (2.0 / 3.0))
    b = jnp.where(up, b, -b)
    signed = jnp.where(up, half, -half)
    return (c - signed - 3.0 * b) * (1.0 / 12.0), (signed - 3.0 * b) * (1.0 / 12.0), 6.0 * b


def face_value(q0, q1, q2, q3):
    return 7.0 * (q1 + q2) - (q0 + q3)


def face_flux(mid, below, above, q_below, q_above, ka, ku, kq):
    up = kq >= 0.0
    return ka * mid + ku * jnp.where(up, below, above) + kq * jnp.where(up, q_below, q_above)


def kernel(
    x_ref, c1_ref, c2_ref, w_ref, f_ref, o_ref,
    x_vmem, w_vmem, send, recv, c_tmp, c_send, c_recv, raw, flags,
    fa, fb, halo_low, halo_high, edge_send, edge_recv,
    k1, k2, mix_send, mix_recv, columns, matrix, mixed,
    a_ssem, a_rsem, c_ssem, c_rsem, h_ssem, h_rsem, e_ssem, e_rsem, m_ssem, m_rsem, d_ssem, d_rsem, l_sem, i_sem,
):
    t = lax.axis_index("tile")
    l = lax.axis_index("lev")
    div, rem = lax.div, lax.rem
    ring = div(t, 8)
    yc = rem(t, 8)
    hi = div(ring, 4)
    x = rem(ring, 4)
    z = hi * 4 + l
    group = rem(l + 2, 4)
    eighth = div(rem(z + 6, 8), 4) * 4 + x

    def at(zz, xx):
        return {"tile": (div(zz, 4) * 4 + xx) * 8 + yc, "lev": rem(zz, 4)}

    low = {"tile": ring * 8 + rem(yc + 7, 8), "lev": l}
    high = {"tile": ring * 8 + rem(yc + 1, 8), "lev": l}

    pending = {}

    def begin(key, start, sent, arrived):
        start()
        pending[key] = [arrived, sent]

    def left(*keys):
        for key in keys:
            pending[key][1]()
            pending[key][1] = lambda: None

    def arrive(*keys):
        for key in keys:
            pending[key][0]()
            pending[key][0] = None

    barrier = pltpu.get_barrier_semaphore()
    greeted = [at(rem(z + dz, 8), rem(x + dx, 4)) for dz in (2, 6) for dx in range(4)]
    greeted += [at(rem(z + 1, 8), x), at(rem(z + 7, 8), x), low, high]
    for device in greeted:
        pl.semaphore_signal(barrier, inc=1, device_id=device, device_id_type=MESH)
    x_load = pltpu.make_async_copy(x_ref.at[0], x_vmem, i_sem.at[0])
    w_load = pltpu.make_async_copy(w_ref.at[0], w_vmem, i_sem.at[1])
    x_load.start()
    w_load.start()

    flip_i = f_ref[0, 0]
    flip_j = f_ref[0, 1]
    c_tmp[...] = jnp.zeros((128, 128), jnp.float32)
    for i in range(8):
        c_tmp[8 * i:8 * i + 8, 0:LEV] = c1_ref[0, i]
        c_tmp[64 + 8 * i:72 + 8 * i, 0:LEV] = c2_ref[0, i]
    turned = c_tmp[...].T
    c_send[...] = turned[0:24]
    c_send[18:19, :] = jnp.full((1, 128), flip_i, jnp.int32).astype(jnp.float32)
    c_send[19:20, :] = jnp.full((1, 128), flip_j, jnp.int32).astype(jnp.float32)

    x_load.wait()
    turn = jnp.full((8, 128), flip_j, jnp.int32) == 1

    def pack(n, carry):
        levels = [2 * n, 2 * n + 1]
        for lev in levels:
            for i in range(8):
                fb[SUBSTEPS - 1, lev, pl.ds(i, 8, stride=8), :] = x_vmem[i + flip_i * (7 - 2 * i), lev]
        for lev in levels:
            rows = [fb[SUBSTEPS - 1, lev, 8 * j:8 * j + 8, :] for j in range(8)]
            rows = [jnp.where(turn, rows[7 - j], rows[j]) for j in range(8)]
            for d, v in enumerate(pick_blocks(turn_blocks(rows))):
                send[d, lev] = v
        return carry

    lax.fori_loop(0, LEV // 2, pack, 0)

    pl.semaphore_wait(barrier, len(greeted))

    def block_of(zz, xx):
        return div(rem(zz + 6, 8), 4) * 4 + xx

    def ring_copy(o, sending):
        dz, dx = (2, 6)[o // 4], o % 4
        if sending:
            return rem(z + dz, 8), rem(x + dx, 4), ring
        zs, xs = rem(z + 8 - dz, 8), rem(x + 4 - dx, 4)
        return zs, xs, div(zs, 4) * 4 + xs

    def c_copy(o, sending=True):
        zz, xx, slot = ring_copy(o, sending)
        return pltpu.make_async_remote_copy(
            src_ref=c_send, dst_ref=c_recv.at[pl.ds(slot * 24, 24)],
            send_sem=c_ssem.at[o], recv_sem=c_rsem.at[o], device_id=at(zz, xx), device_id_type=MESH)

    def a_copy(o, ch, sending=True):
        first, count = CHUNKS[ch]
        zz, xx, slot = ring_copy(o, sending)
        return pltpu.make_async_remote_copy(
            src_ref=send.at[block_of(zz, xx), pl.ds(first, count)], dst_ref=recv.at[slot, pl.ds(first, count)],
            send_sem=a_ssem.at[o, ch], recv_sem=a_rsem.at[o, ch], device_id=at(zz, xx), device_id_type=MESH)

    order = [0, 4, 1, 5, 2, 6, 3, 7]
    for o in order:
        begin(("c", o), c_copy(o).start, c_copy(o).wait_send, c_copy(o, False).wait_recv)
    def exchange(ch):
        for o in order:
            begin(("a", ch, o), a_copy(o, ch).start, a_copy(o, ch).wait_send, a_copy(o, ch, False).wait_recv)

    exchange(0)
    w_load.wait()
    diagonal = jnp.where(
        lax.broadcasted_iota(jnp.int32, (72, 72), 0) == lax.broadcasted_iota(jnp.int32, (72, 72), 1), 0.6, 0.0)

    def prepare(cell, carry):
        s, j = cell // 8, cell % 8
        w = w_vmem[s, j]
        total = jnp.sum(w, axis=-1, keepdims=True)
        matrix[cell] = 0.4 * (w / total) + diagonal
        return carry

    lax.fori_loop(0, 16, prepare, 0)

    arrive(*(("c", o) for o in range(8)))
    spread = (
        lax.broadcasted_iota(jnp.int32, (24, 128), 0) % 8 == lax.broadcasted_iota(jnp.int32, (24, 128), 1) // 16
    ).astype(jnp.float32).astype(jnp.bfloat16)

    def spread_level(lev):
        v = c_recv[pl.ds(lev, 8, stride=24), :]
        p0 = v.astype(jnp.bfloat16).astype(jnp.float32)
        p1 = (v - p0).astype(jnp.bfloat16).astype(jnp.float32)
        p2 = v - p0 - p1
        parts = jnp.concatenate([p0, p1, p2], axis=0).astype(jnp.bfloat16)
        return lax.dot_general(parts, spread, (((0,), (0,)), ((), ())), preferred_element_type=jnp.float32)

    def courant(first, width, n, carry):
        levels = [first + width * n + u for u in range(width)]
        for u, lev in enumerate(levels):
            wide = spread_level(lev)
            for i in range(8):
                for n, value in enumerate(coefficients(wide[8 * i:8 * i + 8])):
                    k1[n, lev, 8 * i + 8:8 * i + 16, :] = value
                    if i == 7:
                        k1[n, lev, 0:8, :] = pltpu.roll(value, 16, 1)
                raw[u, pl.ds(i, 8, stride=8), :] = wide[64 + 8 * i:72 + 8 * i]
        for u, lev in enumerate(levels):
            for j in range(8):
                for n, value in enumerate(coefficients(raw[u, 8 * j:8 * j + 8, :])):
                    k2[n, lev, 8 * j + 8:8 * j + 16, :] = value
            edge_send[lev] = raw[u, 56:64, :]
        return carry

    def edge_copy(ch):
        part = pl.ds(*CHUNKS[ch])
        return pltpu.make_async_remote_copy(
            src_ref=edge_send.at[part], dst_ref=edge_recv.at[part],
            send_sem=e_ssem.at[ch], recv_sem=e_rsem.at[ch], device_id=high, device_id_type=MESH)

    def courant_chunk(ch):
        first, count = CHUNKS[ch]
        width = 3 if count % 3 == 0 else 2
        lax.fori_loop(0, count // width, functools.partial(courant, first, width), 0)
        edge = edge_copy(ch)
        begin(("e", ch), edge.start, edge.wait_send, edge.wait_recv)

    roll_low = jnp.where(yc == 0, 16, 0)
    roll_high = jnp.where(yc == 7, 112, 0)
    arrival_turn = [16 * rem(slot + 8 - eighth, 8) for slot in range(8)]
    column_turn = [16 * rem(slot + 8 - ring, 8) for slot in range(8)]

    def unpack(ch):
        first, count = CHUNKS[ch]
        arrive(*(("a", ch, o) for o in range(8)))

        def some(n, carry):
            levels = [first + 2 * n, first + 2 * n + 1]
            for lev in levels:
                rows = pick_blocks([pltpu.roll(recv[slot, lev], arrival_turn[slot], 1) for slot in range(8)])
                for j, v in enumerate(turn_back(rows)):
                    fa[lev, pl.ds(j, 8, stride=8), :] = v
            return carry

        lax.fori_loop(0, count // 2, some, 0)

    def advance(q, low_cells, high_cells, k, lev):
        e = low_cells + q + high_cells
        a = [face_value(*e[n:n + 4]) for n in range(11)]
        flux = [
            face_flux(a[f + 1], a[f], a[f + 2], e[f + 2], e[f + 3], *(k[n, lev, 8 * f:8 * f + 8, :] for n in range(3)))
            for f in range(9)]
        return [q[n] - (flux[n + 1] - flux[n]) for n in range(8)]

    def sweep_first(step, ch):
        first, count = CHUNKS[ch]

        def level(lev):
            q = [fa[lev, 8 * i:8 * i + 8, :] for i in range(8)]
            return advance(q, [pltpu.roll(v, 16, 1) for v in q[5:]], [pltpu.roll(v, 112, 1) for v in q[:3]], k1, lev)

        def some(n, carry):
            levels = [first + n * UNROLL + k for k in range(UNROLL)]
            new = [level(lev) for lev in levels]
            for lev, rows in zip(levels, new):
                for i in range(8):
                    fb[step, lev, pl.ds(i, 8, stride=8), :] = rows[i]
            return carry

        lax.fori_loop(0, count // UNROLL, some, 0)

    def halo_copies(step, ch):
        first, count = CHUNKS[ch]
        return (
            pltpu.make_async_remote_copy(
                src_ref=fb.at[step, pl.ds(first, count), pl.ds(40, 24)], dst_ref=halo_low.at[step, pl.ds(first, count)],
                send_sem=h_ssem.at[0, step, ch], recv_sem=h_rsem.at[0, step, ch], device_id=high, device_id_type=MESH),
            pltpu.make_async_remote_copy(
                src_ref=fb.at[step, pl.ds(first, count), pl.ds(0, 24)], dst_ref=halo_high.at[step, pl.ds(first, count)],
                send_sem=h_ssem.at[1, step, ch], recv_sem=h_rsem.at[1, step, ch], device_id=low, device_id_type=MESH),
        )

    def sweep_second(step, ch):
        first, count = CHUNKS[ch]
        last = step == SUBSTEPS - 1

        def level(lev):
            q = [fb[step, lev, 8 * j:8 * j + 8, :] for j in range(8)]
            new = advance(
                q, [pltpu.roll(halo_low[step, lev, 8 * j:8 * j + 8, :], roll_low, 1) for j in range(3)],
                [pltpu.roll(halo_high[step, lev, 8 * j:8 * j + 8, :], roll_high, 1) for j in range(3)], k2, lev)
            if last:
                back = flags[1] > 0.5
                new = [jnp.where(back, new[7 - j], new[j]) for j in range(8)]
            return new

        def some(n, carry):
            levels = [first + n * UNROLL + k for k in range(UNROLL)]
            new = [level(lev) for lev in levels]
            for lev, rows in zip(levels, new):
                for j in range(8):
                    fa[lev, pl.ds(j, 8, stride=8), :] = rows[j]
            return carry

        lax.fori_loop(0, count // UNROLL, some, 0)

    def edge_chunk(ch):
        first, count = CHUNKS[ch]
        arrive(("e", ch))

        def some(n, carry):
            for lev in [first + 2 * n, first + 2 * n + 1]:
                for n, value in enumerate(coefficients(pltpu.roll(edge_recv[lev], roll_low, 1))):
                    k2[n, lev, 0:8, :] = value
            return carry

        lax.fori_loop(0, count // 2, some, 0)

    def mix_pack(ch):
        groups = GROUPS[ch]

        def one(r, carry):
            back = flags[0] > 0.5
            for m in groups:
                rows = []
                for k in range(8):
                    lev, i = 4 * m + k // 2, 2 * r + k % 2
                    if lev < LEV:
                        here = fa[lev, pl.ds(pl.multiple_of(8 * i, 8), 8), :]
                        there = fa[lev, pl.ds(pl.multiple_of(56 - 8 * i, 8), 8), :]
                        rows.append(jnp.where(back, there, here))
                    else:
                        rows.append(jnp.zeros((8, 128), jnp.float32))
                for k, v in enumerate(pick_blocks(turn_blocks(rows))):
                    mix_send[k * 4 + r, m] = v
            return carry

        lax.fori_loop(0, 4, one, 0)

    def m_copy(o, ch):
        dz, dx = (o // 4, o % 4) if isinstance(o, int) else (div(o, 4), rem(o, 4))
        zd, xd = rem(z + dz, 8), rem(x + dx, 4)
        part = pl.ds(GROUPS[ch][0], len(GROUPS[ch]))
        return pltpu.make_async_remote_copy(
            src_ref=mix_send.at[(div(zd, 4) * 4 + xd) * 4 + rem(zd, 4), part], dst_ref=mix_recv.at[group * 8 + eighth, part],
            send_sem=m_ssem.at[ch, o], recv_sem=m_rsem.at[ch, o], device_id=at(zd, xd), device_id_type=MESH)

    def m_arrival(o, ch):
        zs, xs = rem(z + 8 - div(o, 4), 8), rem(x + 4 - rem(o, 4), 4)
        slot = rem(zs + 2, 4) * 8 + block_of(zs, xs)
        part = pl.ds(GROUPS[ch][0], len(GROUPS[ch]))
        return pltpu.make_async_remote_copy(
            src_ref=mix_send.at[0, part], dst_ref=mix_recv.at[slot, part],
            send_sem=m_ssem.at[ch, o], recv_sem=m_rsem.at[ch, o], device_id=at(zs, xs), device_id_type=MESH)

    own = [
        pltpu.make_async_copy(
            mix_send.at[ring * 4 + l, pl.ds(groups[0], len(groups))],
            mix_recv.at[group * 8 + eighth, pl.ds(groups[0], len(groups))], l_sem.at[2 + ch])
        for ch, groups in enumerate(GROUPS)
    ]

    def segment(step, ch):
        if step == 0:
            unpack(ch)
        else:
            if step == 1:
                edge_chunk(ch)
            arrive(("h", step - 1, ch, 0), ("h", step - 1, ch, 1))
            sweep_second(step - 1, ch)
        if step < SUBSTEPS:
            sweep_first(step, ch)
            for side, copy in enumerate(halo_copies(step, ch)):
                begin(("h", step, ch, side), copy.start, copy.wait_send, copy.wait_recv)

    def others(action):
        def run():
            def one(o, carry):
                action(o)
                return carry

            lax.fori_loop(1, 32, one, 0)

        return run

    def scatter(ch):
        mix_pack(ch)

        def far_first():
            for dz in (4, 3, 5, 2, 6, 1, 7, 0):
                for dx in (2, 1, 3, 0):
                    if dz or dx:
                        m_copy(4 * dz + dx, ch).start()

        begin(
            ("m", ch), far_first,
            others(lambda o: m_copy(o, ch).wait_send()), others(lambda o: m_arrival(o, ch).wait_recv()))
        begin(("own", ch), own[ch].start, lambda: None, own[ch].wait)

    for what, ch, *step in SCHEDULE:
        if what == "send":
            left(*(("a", ch - 1, o) for o in range(8)))
            exchange(ch)
        elif what == "flags":
            for n in range(2):
                flags[n] = spread_level(LEV + n)[0:8]
        elif what == "courant":
            courant_chunk(ch)
        elif what == "scatter":
            scatter(ch)
        else:
            segment(step[0], ch)

    def mix_unpack(ch):
        def one(g, carry):
            for m in GROUPS[ch]:
                rows = pick_blocks([pltpu.roll(mix_recv[g * 8 + k, m], column_turn[k], 1) for k in range(8)])
                rows = turn_back(rows)
                for k in range(8):
                    lev, s = 4 * m + k // 2, k % 2
                    if lev < LEV:
                        columns[s, pl.ds(pl.multiple_of((g * LEV + lev) * 8, 8), 8), :] = rows[k]
            return carry

        lax.fori_loop(0, 4, one, 0)

    for ch in range(NCH):
        arrive(("m", ch), ("own", ch))
        mix_unpack(ch)

    def d_copy(s, o):
        to = rem(l + o, 4)
        return pltpu.make_async_remote_copy(
            src_ref=mixed.at[s, pl.ds(to * 144, 144)], dst_ref=o_ref.at[0, 2 * l + s],
            send_sem=d_ssem.at[s, o], recv_sem=d_rsem.at[s, o], device_id={"tile": t, "lev": to}, device_id_type=MESH)

    def d_arrival(s, o):
        source = rem(l + 4 - o, 4)
        return pltpu.make_async_remote_copy(
            src_ref=mixed.at[s, pl.ds(0, 144)], dst_ref=o_ref.at[0, 2 * source + s],
            send_sem=d_ssem.at[s, o], recv_sem=d_rsem.at[s, o], device_id={"tile": t, "lev": source}, device_id_type=MESH)

    def mix_row(s):
        def cell(j):
            v = columns[s, pl.ds(j, 72, stride=8), :]
            v_hi = v.astype(jnp.bfloat16)
            v_lo = (v - v_hi.astype(jnp.float32)).astype(jnp.bfloat16)
            m = matrix[s * 8 + j]
            m_hi = m.astype(jnp.bfloat16)
            m_lo = (m - m_hi.astype(jnp.float32)).astype(jnp.bfloat16)
            dot = lambda a, b: jnp.dot(a, b, preferred_element_type=jnp.float32)
            out = dot(m_hi, v_hi) + (dot(m_hi, v_lo) + dot(m_lo, v_hi))
            mixed[s, pl.ds(j, 72, stride=8), :] = out

        def some(n, carry):
            for j in range(CELLS):
                cell(CELLS * n + j)
            return carry

        lax.fori_loop(0, 8 // CELLS, some, 0)

    for s in range(2):
        mix_row(s)
        for o in (2, 3, 1):
            begin(("d", s, o), d_copy(s, o).start, d_copy(s, o).wait_send, d_arrival(s, o).wait_recv)
        local = pltpu.make_async_copy(mixed.at[s, pl.ds(l * 144, 144)], o_ref.at[0, 2 * l + s], l_sem.at[s])
        begin(("local", s), local.start, lambda: None, local.wait)

    for arrived, sent in pending.values():
        if arrived is not None:
            arrived()
        sent()


def solution(mesh):
    f32 = jnp.float32

    def on_device(tracers, courant_first, courant_second, weights, frame_flip):
        vmem = pl.BlockSpec(memory_space=pltpu.VMEM)
        hbm = pl.BlockSpec(memory_space=pl.ANY)
        dma = pltpu.SemaphoreType.DMA
        rows = jnp.transpose(tracers, (0, 1, 3, 2, 4)).reshape(1, 8, LEV, 8, 128)
        out = pl.pallas_call(
            kernel,
            out_shape=jax.ShapeDtypeStruct((1, 8, LEV * 8, 128), f32),
            in_specs=[hbm, vmem, vmem, hbm, pl.BlockSpec(memory_space=pltpu.SMEM)],
            out_specs=hbm,
            scratch_shapes=[
                pltpu.VMEM((8, LEV, 8, 128), f32),
                pltpu.VMEM((2, 8, 72, 72), f32),
                pltpu.VMEM((8, LEV, 8, 128), f32),
                pltpu.VMEM((8, LEV, 8, 128), f32),
                pltpu.VMEM((128, 128), f32),
                pltpu.VMEM((24, 128), f32),
                pltpu.VMEM((192, 128), f32),
                pltpu.VMEM((3, 64, 128), f32),
                pltpu.VMEM((2, 8, 128), f32),
                pltpu.VMEM((LEV, 64, 128), f32),
                pltpu.VMEM((SUBSTEPS, LEV, 64, 128), f32),
                pltpu.VMEM((SUBSTEPS, LEV, 24, 128), f32),
                pltpu.VMEM((SUBSTEPS, LEV, 24, 128), f32),
                pltpu.VMEM((LEV, 8, 128), f32),
                pltpu.VMEM((LEV, 8, 128), f32),
                pltpu.VMEM((3, LEV, 72, 128), f32),
                pltpu.VMEM((3, LEV, 72, 128), f32),
                pltpu.VMEM((32, 5, 8, 128), f32),
                pltpu.VMEM((32, 5, 8, 128), f32),
                pltpu.VMEM((2, 72 * 8, 128), f32),
                pltpu.VMEM((16, 72, 72), f32),
                pltpu.VMEM((2, 72 * 8, 128), f32),
                dma((8, NCH)), dma((8, NCH)),
                dma((8,)), dma((8,)),
                dma((2, SUBSTEPS, NCH)), dma((2, SUBSTEPS, NCH)),
                dma((NCH,)), dma((NCH,)),
                dma((NCH, 32)), dma((NCH, 32)),
                dma((2, 4)), dma((2, 4)),
                dma((2 + NCH,)),
                dma((2,)),
            ],
            compiler_params=pltpu.CompilerParams(collective_id=0, has_side_effects=True),
        )(rows, courant_first, courant_second, weights, frame_flip)
        return jnp.transpose(out.reshape(1, 8, LEV, 8, 128), (0, 1, 3, 2, 4))

    return jax.shard_map(
        on_device,
        mesh=mesh,
        in_specs=(
            P("tile", None, None, "lev", None),
            P("tile", None, None, "lev"),
            P("tile", None, None, "lev"),
            P("tile", "lev", None, None, None),
            P("tile", None),
        ),
        out_specs=P("tile", None, None, "lev", None),
        check_vma=False,
    )
```

```python
import functools

import jax
import jax.numpy as jnp
from jax import lax
from jax.experimental import pallas as pl
from jax.experimental.pallas import tpu as pltpu
from jax.sharding import PartitionSpec as P

MESH = pl.DeviceIdType.MESH
SUBSTEPS = 3
LEV = 18
CHUNKS = ((0, 8), (8, 4), (12, 6))
NCH = len(CHUNKS)
SCHEDULE = (
    ("courant", 0), ("send", 1), ("step", 0, 0), ("courant", 1), ("send", 2), ("courant", 2), ("flags", 0),
    ("step", 0, 1), ("step", 1, 0), ("step", 0, 2), ("step", 1, 1), ("step", 2, 0), ("step", 0, 3), ("scatter", 0),
    ("step", 1, 2), ("step", 2, 1), ("step", 1, 3), ("scatter", 1), ("step", 2, 2), ("step", 2, 3), ("scatter", 2),
)
GROUPS = tuple(tuple(range(first // 4, (first + count + 3) // 4)) for first, count in CHUNKS)
UNROLL = 2
CELLS = 4


def turn_blocks(rows):
    return [pltpu.roll(v, 16 * k, 1) if k else v for k, v in enumerate(rows)]


def pick_blocks(rows):
    block = lax.broadcasted_iota(jnp.int32, (8, 128), 1) // 16
    rows = [rows[(8 - b) % 8] for b in range(8)]
    for m in (1, 2, 4):
        other = (block & m) != 0
        rows = [jnp.where(other, rows[(b + 8 - m) % 8], rows[b]) for b in range(8)]
    return rows


def turn_back(rows):
    return [pltpu.roll(v, 128 - 16 * b, 1) if b else v for b, v in enumerate(rows)]


def coefficients(c):
    up = c >= 0.0
    half = 0.5 * c * c
    b = half * (1.0 - jnp.abs(c) * (2.0 / 3.0))
    b = jnp.where(up, b, -b)
    signed = jnp.where(up, half, -half)
    return (c - signed - 3.0 * b) * (1.0 / 12.0), (signed - 3.0 * b) * (1.0 / 12.0), 6.0 * b


def face_value(q0, q1, q2, q3):
    return 7.0 * (q1 + q2) - (q0 + q3)


def face_flux(mid, below, above, q_below, q_above, ka, ku, kq):
    up = kq >= 0.0
    return ka * mid + ku * jnp.where(up, below, above) + kq * jnp.where(up, q_below, q_above)


def kernel(
    x_ref, c1_ref, c2_ref, w_ref, f_ref, o_ref,
    x_vmem, c_vmem, w_vmem, send, recv, c_tmp, c_send, c_recv, raw, flags,
    fa, fb, halo_low, halo_high, edge_send, edge_recv,
    k1, k2, mix_send, mix_recv, columns, matrix, mixed,
    a_ssem, a_rsem, c_ssem, c_rsem, h_ssem, h_rsem, e_ssem, e_rsem, m_ssem, m_rsem, d_ssem, d_rsem, l_sem, i_sem,
):
    t = lax.axis_index("tile")
    l = lax.axis_index("lev")
    div, rem = lax.div, lax.rem
    ring = div(t, 8)
    yc = rem(t, 8)
    hi = div(ring, 4)
    x = rem(ring, 4)
    z = hi * 4 + l
    group = rem(l + 2, 4)
    eighth = div(rem(z + 6, 8), 4) * 4 + x

    def at(zz, xx):
        return {"tile": (div(zz, 4) * 4 + xx) * 8 + yc, "lev": rem(zz, 4)}

    low = {"tile": ring * 8 + rem(yc + 7, 8), "lev": l}
    high = {"tile": ring * 8 + rem(yc + 1, 8), "lev": l}

    pending = {}

    def begin(key, start, sent, arrived):
        start()
        pending[key] = [arrived, sent]

    def left(*keys):
        for key in keys:
            pending[key][1]()
            pending[key][1] = lambda: None

    def arrive(*keys):
        for key in keys:
            pending[key][0]()
            pending[key][0] = None

    barrier = pltpu.get_barrier_semaphore()
    greeted = [at(rem(z + dz, 8), rem(x + dx, 4)) for dz in (2, 6) for dx in range(4)]
    greeted += [at(rem(z + 1, 8), x), at(rem(z + 7, 8), x), low, high]
    for device in greeted:
        pl.semaphore_signal(barrier, inc=1, device_id=device, device_id_type=MESH)
    x_load = pltpu.make_async_copy(x_ref.at[0], x_vmem, i_sem.at[0])
    w_load = pltpu.make_async_copy(w_ref.at[0], w_vmem, i_sem.at[1])
    c_load = [pltpu.make_async_copy(ref.at[0], c_vmem.at[n], i_sem.at[2 + n]) for n, ref in enumerate((c1_ref, c2_ref))]
    c_load[0].start()
    c_load[1].start()
    x_load.start()
    w_load.start()

    flip_i = f_ref[0, 0]
    flip_j = f_ref[0, 1]
    c_tmp[...] = jnp.zeros((128, 128), jnp.float32)
    for n in range(2):
        c_load[n].wait()
        for i in range(8):
            c_tmp[64 * n + 8 * i:64 * n + 8 * i + 8, 0:LEV] = c_vmem[n, i]
    turned = c_tmp[...].T
    c_send[...] = turned[0:24]
    c_send[18:19, :] = jnp.full((1, 128), flip_i, jnp.int32).astype(jnp.float32)
    c_send[19:20, :] = jnp.full((1, 128), flip_j, jnp.int32).astype(jnp.float32)

    x_load.wait()
    turn = jnp.full((8, 128), flip_j, jnp.int32) == 1

    def pack(n, carry):
        levels = [2 * n, 2 * n + 1]
        for lev in levels:
            for i in range(8):
                fb[SUBSTEPS - 1, lev, pl.ds(i, 8, stride=8), :] = x_vmem[i + flip_i * (7 - 2 * i), lev]
        for lev in levels:
            rows = [fb[SUBSTEPS - 1, lev, 8 * j:8 * j + 8, :] for j in range(8)]
            rows = [jnp.where(turn, rows[7 - j], rows[j]) for j in range(8)]
            for d, v in enumerate(pick_blocks(turn_blocks(rows))):
                send[d, lev] = v
        return carry

    lax.fori_loop(0, LEV // 2, pack, 0)

    pl.semaphore_wait(barrier, len(greeted))

    def block_of(zz, xx):
        return div(rem(zz + 6, 8), 4) * 4 + xx

    def ring_copy(o, sending):
        dz, dx = (2, 6)[o // 4], o % 4
        if sending:
            return rem(z + dz, 8), rem(x + dx, 4), ring
        zs, xs = rem(z + 8 - dz, 8), rem(x + 4 - dx, 4)
        return zs, xs, div(zs, 4) * 4 + xs

    def c_copy(o, sending=True):
        zz, xx, slot = ring_copy(o, sending)
        return pltpu.make_async_remote_copy(
            src_ref=c_send, dst_ref=c_recv.at[pl.ds(slot * 24, 24)],
            send_sem=c_ssem.at[o], recv_sem=c_rsem.at[o], device_id=at(zz, xx), device_id_type=MESH)

    def a_copy(o, ch, sending=True):
        first, count = CHUNKS[ch]
        zz, xx, slot = ring_copy(o, sending)
        return pltpu.make_async_remote_copy(
            src_ref=send.at[block_of(zz, xx), pl.ds(first, count)], dst_ref=recv.at[slot, pl.ds(first, count)],
            send_sem=a_ssem.at[o, ch], recv_sem=a_rsem.at[o, ch], device_id=at(zz, xx), device_id_type=MESH)

    order = [2, 6, 1, 5, 3, 7, 0, 4]
    for o in order:
        begin(("c", o), c_copy(o).start, c_copy(o).wait_send, c_copy(o, False).wait_recv)
    def exchange(ch):
        for o in order:
            begin(("a", ch, o), a_copy(o, ch).start, a_copy(o, ch).wait_send, a_copy(o, ch, False).wait_recv)

    exchange(0)
    w_load.wait()
    diagonal = jnp.where(
        lax.broadcasted_iota(jnp.int32, (72, 72), 0) == lax.broadcasted_iota(jnp.int32, (72, 72), 1), 0.6, 0.0)

    def prepare(cell, carry):
        s, j = cell // 8, cell % 8
        w = w_vmem[s, j]
        total = jnp.sum(w, axis=-1, keepdims=True)
        matrix[cell] = 0.4 * (w / total) + diagonal
        return carry

    lax.fori_loop(0, 16, prepare, 0)

    arrive(*(("c", o) for o in range(8)))
    spread = (
        lax.broadcasted_iota(jnp.int32, (24, 128), 0) % 8 == lax.broadcasted_iota(jnp.int32, (24, 128), 1) // 16
    ).astype(jnp.float32).astype(jnp.bfloat16)

    def spread_level(lev):
        v = c_recv[pl.ds(lev, 8, stride=24), :]
        p0 = v.astype(jnp.bfloat16).astype(jnp.float32)
        p1 = (v - p0).astype(jnp.bfloat16).astype(jnp.float32)
        p2 = v - p0 - p1
        parts = jnp.concatenate([p0, p1, p2], axis=0).astype(jnp.bfloat16)
        return lax.dot_general(parts, spread, (((0,), (0,)), ((), ())), preferred_element_type=jnp.float32)

    def courant(first, width, n, carry):
        levels = [first + width * n + u for u in range(width)]
        for u, lev in enumerate(levels):
            wide = spread_level(lev)
            for i in range(8):
                for n, value in enumerate(coefficients(wide[8 * i:8 * i + 8])):
                    k1[n, lev, 8 * i + 8:8 * i + 16, :] = value
                    if i == 7:
                        k1[n, lev, 0:8, :] = pltpu.roll(value, 16, 1)
                raw[u, pl.ds(i, 8, stride=8), :] = wide[64 + 8 * i:72 + 8 * i]
        for u, lev in enumerate(levels):
            for j in range(8):
                for n, value in enumerate(coefficients(raw[u, 8 * j:8 * j + 8, :])):
                    k2[n, lev, 8 * j + 8:8 * j + 16, :] = value
            edge_send[lev] = raw[u, 56:64, :]
        return carry

    def edge_copy(ch):
        part = pl.ds(*CHUNKS[ch])
        return pltpu.make_async_remote_copy(
            src_ref=edge_send.at[part], dst_ref=edge_recv.at[part],
            send_sem=e_ssem.at[ch], recv_sem=e_rsem.at[ch], device_id=high, device_id_type=MESH)

    def courant_chunk(ch):
        first, count = CHUNKS[ch]
        width = 3 if count % 3 == 0 else 2
        lax.fori_loop(0, count // width, functools.partial(courant, first, width), 0)
        edge = edge_copy(ch)
        begin(("e", ch), edge.start, edge.wait_send, edge.wait_recv)

    roll_low = jnp.where(yc == 0, 16, 0)
    roll_high = jnp.where(yc == 7, 112, 0)
    arrival_turn = [16 * rem(slot + 8 - eighth, 8) for slot in range(8)]
    column_turn = [16 * rem(slot + 8 - ring, 8) for slot in range(8)]

    def unpack(ch):
        first, count = CHUNKS[ch]
        arrive(*(("a", ch, o) for o in range(8)))

        def some(n, carry):
            levels = [first + 2 * n, first + 2 * n + 1]
            for lev in levels:
                rows = pick_blocks([pltpu.roll(recv[slot, lev], arrival_turn[slot], 1) for slot in range(8)])
                for j, v in enumerate(turn_back(rows)):
                    fa[lev, pl.ds(j, 8, stride=8), :] = v
            return carry

        lax.fori_loop(0, count // 2, some, 0)

    def advance(q, low_cells, high_cells, k, lev):
        e = low_cells + q + high_cells
        a = [face_value(*e[n:n + 4]) for n in range(11)]
        flux = [
            face_flux(a[f + 1], a[f], a[f + 2], e[f + 2], e[f + 3], *(k[n, lev, 8 * f:8 * f + 8, :] for n in range(3)))
            for f in range(9)]
        return [q[n] - (flux[n + 1] - flux[n]) for n in range(8)]

    def sweep_first(step, ch):
        first, count = CHUNKS[ch]

        def level(lev):
            q = [fa[lev, 8 * i:8 * i + 8, :] for i in range(8)]
            return advance(q, [pltpu.roll(v, 16, 1) for v in q[5:]], [pltpu.roll(v, 112, 1) for v in q[:3]], k1, lev)

        def some(n, carry):
            levels = [first + n * UNROLL + k for k in range(UNROLL)]
            new = [level(lev) for lev in levels]
            for lev, rows in zip(levels, new):
                for i in range(8):
                    fb[step, lev, pl.ds(i, 8, stride=8), :] = rows[i]
            return carry

        lax.fori_loop(0, count // UNROLL, some, 0)

    def halo_copies(step, ch):
        first, count = CHUNKS[ch]
        return (
            pltpu.make_async_remote_copy(
                src_ref=fb.at[step, pl.ds(first, count), pl.ds(40, 24)], dst_ref=halo_low.at[step, pl.ds(first, count)],
                send_sem=h_ssem.at[0, step, ch], recv_sem=h_rsem.at[0, step, ch], device_id=high, device_id_type=MESH),
            pltpu.make_async_remote_copy(
                src_ref=fb.at[step, pl.ds(first, count), pl.ds(0, 24)], dst_ref=halo_high.at[step, pl.ds(first, count)],
                send_sem=h_ssem.at[1, step, ch], recv_sem=h_rsem.at[1, step, ch], device_id=low, device_id_type=MESH),
        )

    def sweep_second(step, ch):
        first, count = CHUNKS[ch]
        last = step == SUBSTEPS - 1

        def level(lev):
            q = [fb[step, lev, 8 * j:8 * j + 8, :] for j in range(8)]
            new = advance(
                q, [pltpu.roll(halo_low[step, lev, 8 * j:8 * j + 8, :], roll_low, 1) for j in range(3)],
                [pltpu.roll(halo_high[step, lev, 8 * j:8 * j + 8, :], roll_high, 1) for j in range(3)], k2, lev)
            if last:
                back = flags[1] > 0.5
                new = [jnp.where(back, new[7 - j], new[j]) for j in range(8)]
            return new

        def some(n, carry):
            levels = [first + n * UNROLL + k for k in range(UNROLL)]
            new = [level(lev) for lev in levels]
            for lev, rows in zip(levels, new):
                for j in range(8):
                    fa[lev, pl.ds(j, 8, stride=8), :] = rows[j]
            return carry

        lax.fori_loop(0, count // UNROLL, some, 0)

    def edge_chunk(ch):
        first, count = CHUNKS[ch]
        arrive(("e", ch))

        def some(n, carry):
            for lev in [first + 2 * n, first + 2 * n + 1]:
                for n, value in enumerate(coefficients(pltpu.roll(edge_recv[lev], roll_low, 1))):
                    k2[n, lev, 0:8, :] = value
            return carry

        lax.fori_loop(0, count // 2, some, 0)

    def mix_pack(ch):
        groups = GROUPS[ch]

        def one(r, carry):
            back = flags[0] > 0.5
            for m in groups:
                rows = []
                for k in range(8):
                    lev, i = 4 * m + k // 2, 2 * r + k % 2
                    if lev < LEV:
                        here = fa[lev, pl.ds(pl.multiple_of(8 * i, 8), 8), :]
                        there = fa[lev, pl.ds(pl.multiple_of(56 - 8 * i, 8), 8), :]
                        rows.append(jnp.where(back, there, here))
                    else:
                        rows.append(jnp.zeros((8, 128), jnp.float32))
                for k, v in enumerate(pick_blocks(turn_blocks(rows))):
                    mix_send[k * 4 + r, m] = v
            return carry

        lax.fori_loop(0, 4, one, 0)

    def m_copy(o, ch):
        dz, dx = (o // 4, o % 4) if isinstance(o, int) else (div(o, 4), rem(o, 4))
        zd, xd = rem(z + dz, 8), rem(x + dx, 4)
        part = pl.ds(GROUPS[ch][0], len(GROUPS[ch]))
        return pltpu.make_async_remote_copy(
            src_ref=mix_send.at[(div(zd, 4) * 4 + xd) * 4 + rem(zd, 4), part], dst_ref=mix_recv.at[group * 8 + eighth, part],
            send_sem=m_ssem.at[ch, o], recv_sem=m_rsem.at[ch, o], device_id=at(zd, xd), device_id_type=MESH)

    def m_arrival(o, ch):
        zs, xs = rem(z + 8 - div(o, 4), 8), rem(x + 4 - rem(o, 4), 4)
        slot = rem(zs + 2, 4) * 8 + block_of(zs, xs)
        part = pl.ds(GROUPS[ch][0], len(GROUPS[ch]))
        return pltpu.make_async_remote_copy(
            src_ref=mix_send.at[0, part], dst_ref=mix_recv.at[slot, part],
            send_sem=m_ssem.at[ch, o], recv_sem=m_rsem.at[ch, o], device_id=at(zs, xs), device_id_type=MESH)

    own = [
        pltpu.make_async_copy(
            mix_send.at[ring * 4 + l, pl.ds(groups[0], len(groups))],
            mix_recv.at[group * 8 + eighth, pl.ds(groups[0], len(groups))], l_sem.at[2 + ch])
        for ch, groups in enumerate(GROUPS)
    ]

    def segment(step, ch):
        if step == 0:
            unpack(ch)
        else:
            if step == 1:
                edge_chunk(ch)
            arrive(("h", step - 1, ch, 0), ("h", step - 1, ch, 1))
            sweep_second(step - 1, ch)
        if step < SUBSTEPS:
            sweep_first(step, ch)
            for side, copy in enumerate(halo_copies(step, ch)):
                begin(("h", step, ch, side), copy.start, copy.wait_send, copy.wait_recv)

    def others(action):
        def run():
            def one(o, carry):
                action(o)
                return carry

            lax.fori_loop(1, 32, one, 0)

        return run

    def scatter(ch):
        mix_pack(ch)

        def far_first():
            for dz in (4, 3, 5, 2, 6, 1, 7, 0):
                for dx in (2, 1, 3, 0):
                    if dz or dx:
                        m_copy(4 * dz + dx, ch).start()

        begin(
            ("m", ch), far_first,
            others(lambda o: m_copy(o, ch).wait_send()), others(lambda o: m_arrival(o, ch).wait_recv()))
        begin(("own", ch), own[ch].start, lambda: None, own[ch].wait)

    for what, ch, *step in SCHEDULE:
        if what == "send":
            left(*(("a", ch - 1, o) for o in range(8)))
            exchange(ch)
        elif what == "flags":
            for n in range(2):
                flags[n] = spread_level(LEV + n)[0:8]
        elif what == "courant":
            courant_chunk(ch)
        elif what == "scatter":
            scatter(ch)
        else:
            segment(step[0], ch)

    def mix_unpack(ch):
        def one(g, carry):
            for m in GROUPS[ch]:
                rows = pick_blocks([pltpu.roll(mix_recv[g * 8 + k, m], column_turn[k], 1) for k in range(8)])
                rows = turn_back(rows)
                for k in range(8):
                    lev, s = 4 * m + k // 2, k % 2
                    if lev < LEV:
                        columns[s, pl.ds(pl.multiple_of((g * LEV + lev) * 8, 8), 8), :] = rows[k]
            return carry

        lax.fori_loop(0, 4, one, 0)

    for ch in range(NCH):
        arrive(("m", ch), ("own", ch))
        mix_unpack(ch)

    def d_copy(s, o):
        to = rem(l + o, 4)
        return pltpu.make_async_remote_copy(
            src_ref=mixed.at[s, pl.ds(to * 144, 144)], dst_ref=o_ref.at[0, 2 * l + s],
            send_sem=d_ssem.at[s, o], recv_sem=d_rsem.at[s, o], device_id={"tile": t, "lev": to}, device_id_type=MESH)

    def d_arrival(s, o):
        source = rem(l + 4 - o, 4)
        return pltpu.make_async_remote_copy(
            src_ref=mixed.at[s, pl.ds(0, 144)], dst_ref=o_ref.at[0, 2 * source + s],
            send_sem=d_ssem.at[s, o], recv_sem=d_rsem.at[s, o], device_id={"tile": t, "lev": source}, device_id_type=MESH)

    def mix_row(s):
        def cell(j):
            v = columns[s, pl.ds(j, 72, stride=8), :]
            v_hi = v.astype(jnp.bfloat16)
            v_lo = (v - v_hi.astype(jnp.float32)).astype(jnp.bfloat16)
            m = matrix[s * 8 + j]
            m_hi = m.astype(jnp.bfloat16)
            m_lo = (m - m_hi.astype(jnp.float32)).astype(jnp.bfloat16)
            dot = lambda a, b: jnp.dot(a, b, preferred_element_type=jnp.float32)
            out = dot(m_hi, v_hi) + (dot(m_hi, v_lo) + dot(m_lo, v_hi))
            mixed[s, pl.ds(j, 72, stride=8), :] = out

        def some(n, carry):
            for j in range(CELLS):
                cell(CELLS * n + j)
            return carry

        lax.fori_loop(0, 8 // CELLS, some, 0)

    for s in range(2):
        mix_row(s)
        for o in (2, 3, 1):
            begin(("d", s, o), d_copy(s, o).start, d_copy(s, o).wait_send, d_arrival(s, o).wait_recv)
        local = pltpu.make_async_copy(mixed.at[s, pl.ds(l * 144, 144)], o_ref.at[0, 2 * l + s], l_sem.at[s])
        begin(("local", s), local.start, lambda: None, local.wait)

    for arrived, sent in pending.values():
        if arrived is not None:
            arrived()
        sent()


def solution(mesh):
    f32 = jnp.float32

    def on_device(tracers, courant_first, courant_second, weights, frame_flip):
        hbm = pl.BlockSpec(memory_space=pl.ANY)
        dma = pltpu.SemaphoreType.DMA
        rows = jnp.transpose(tracers, (0, 1, 3, 2, 4)).reshape(1, 8, LEV, 8, 128)
        out = pl.pallas_call(
            kernel,
            out_shape=jax.ShapeDtypeStruct((1, 8, LEV * 8, 128), f32),
            in_specs=[hbm, hbm, hbm, hbm, pl.BlockSpec(memory_space=pltpu.SMEM)],
            out_specs=hbm,
            scratch_shapes=[
                pltpu.VMEM((8, LEV, 8, 128), f32),
                pltpu.VMEM((2, 8, 8, LEV), f32),
                pltpu.VMEM((2, 8, 72, 72), f32),
                pltpu.VMEM((8, LEV, 8, 128), f32),
                pltpu.VMEM((8, LEV, 8, 128), f32),
                pltpu.VMEM((128, 128), f32),
                pltpu.VMEM((24, 128), f32),
                pltpu.VMEM((192, 128), f32),
                pltpu.VMEM((3, 64, 128), f32),
                pltpu.VMEM((2, 8, 128), f32),
                pltpu.VMEM((LEV, 64, 128), f32),
                pltpu.VMEM((SUBSTEPS, LEV, 64, 128), f32),
                pltpu.VMEM((SUBSTEPS, LEV, 24, 128), f32),
                pltpu.VMEM((SUBSTEPS, LEV, 24, 128), f32),
                pltpu.VMEM((LEV, 8, 128), f32),
                pltpu.VMEM((LEV, 8, 128), f32),
                pltpu.VMEM((3, LEV, 72, 128), f32),
                pltpu.VMEM((3, LEV, 72, 128), f32),
                pltpu.VMEM((32, 5, 8, 128), f32),
                pltpu.VMEM((32, 5, 8, 128), f32),
                pltpu.VMEM((2, 72 * 8, 128), f32),
                pltpu.VMEM((16, 72, 72), f32),
                pltpu.VMEM((2, 72 * 8, 128), f32),
                dma((8, NCH)), dma((8, NCH)),
                dma((8,)), dma((8,)),
                dma((2, SUBSTEPS, NCH)), dma((2, SUBSTEPS, NCH)),
                dma((NCH,)), dma((NCH,)),
                dma((NCH, 32)), dma((NCH, 32)),
                dma((2, 4)), dma((2, 4)),
                dma((2 + NCH,)),
                dma((4,)),
            ],
            compiler_params=pltpu.CompilerParams(collective_id=0, has_side_effects=True),
        )(rows, courant_first, courant_second, weights, frame_flip)
        return jnp.transpose(out.reshape(1, 8, LEV, 8, 128), (0, 1, 3, 2, 4))

    return jax.shard_map(
        on_device,
        mesh=mesh,
        in_specs=(
            P("tile", None, None, "lev", None),
            P("tile", None, None, "lev"),
            P("tile", None, None, "lev"),
            P("tile", "lev", None, None, None),
            P("tile", None),
        ),
        out_specs=P("tile", None, None, "lev", None),
        check_vma=False,
    )
```

```python
import functools

import jax
import jax.numpy as jnp
from jax import lax
from jax.experimental import pallas as pl
from jax.experimental.pallas import tpu as pltpu
from jax.sharding import PartitionSpec as P

MESH = pl.DeviceIdType.MESH
SUBSTEPS = 3
LEV = 18
CHUNKS = ((0, 8), (8, 4), (12, 6))
NCH = len(CHUNKS)
SCHEDULE = (
    ("courant", 0), ("send", 1), ("step", 0, 0), ("courant", 1), ("send", 2), ("courant", 2), ("flags", 0),
    ("step", 0, 1), ("step", 1, 0), ("step", 0, 2), ("step", 1, 1), ("step", 2, 0), ("step", 0, 3), ("scatter", 0),
    ("step", 1, 2), ("step", 2, 1), ("step", 1, 3), ("scatter", 1), ("step", 2, 2), ("step", 2, 3), ("scatter", 2),
)
GROUPS = tuple(tuple(range(first // 4, (first + count + 3) // 4)) for first, count in CHUNKS)
UNROLL = 2
CELLS = 4


def turn_blocks(rows):
    return [pltpu.roll(v, 16 * k, 1) if k else v for k, v in enumerate(rows)]


def pick_blocks(rows):
    block = lax.broadcasted_iota(jnp.int32, (8, 128), 1) // 16
    rows = [rows[(8 - b) % 8] for b in range(8)]
    for m in (1, 2, 4):
        other = (block & m) != 0
        rows = [jnp.where(other, rows[(b + 8 - m) % 8], rows[b]) for b in range(8)]
    return rows


def turn_back(rows):
    return [pltpu.roll(v, 128 - 16 * b, 1) if b else v for b, v in enumerate(rows)]


def coefficients(c):
    up = c >= 0.0
    half = 0.5 * c * c
    b = half * (1.0 - jnp.abs(c) * (2.0 / 3.0))
    b = jnp.where(up, b, -b)
    signed = jnp.where(up, half, -half)
    return (c - signed - 3.0 * b) * (1.0 / 12.0), (signed - 3.0 * b) * (1.0 / 12.0), 6.0 * b


def face_value(q0, q1, q2, q3):
    return 7.0 * (q1 + q2) - (q0 + q3)


def face_flux(mid, below, above, q_below, q_above, ka, ku, kq):
    up = kq >= 0.0
    return ka * mid + ku * jnp.where(up, below, above) + kq * jnp.where(up, q_below, q_above)


def kernel(
    x_ref, c1_ref, c2_ref, w_ref, f_ref, o_ref,
    x_vmem, c_vmem, w_vmem, send, recv, c_tmp, c_send, c_recv, raw, flags,
    fa, fb, halo_low, halo_high, edge_send, edge_recv,
    k1, k2, mix_send, mix_recv, columns, matrix, mixed,
    a_ssem, a_rsem, c_ssem, c_rsem, h_ssem, h_rsem, e_ssem, e_rsem, m_ssem, m_rsem, d_ssem, d_rsem, l_sem, i_sem,
):
    t = lax.axis_index("tile")
    l = lax.axis_index("lev")
    div, rem = lax.div, lax.rem
    ring = div(t, 8)
    yc = rem(t, 8)
    hi = div(ring, 4)
    x = rem(ring, 4)
    z = hi * 4 + l
    group = rem(l + 2, 4)
    eighth = div(rem(z + 6, 8), 4) * 4 + x

    def at(zz, xx):
        return {"tile": (div(zz, 4) * 4 + xx) * 8 + yc, "lev": rem(zz, 4)}

    low = {"tile": ring * 8 + rem(yc + 7, 8), "lev": l}
    high = {"tile": ring * 8 + rem(yc + 1, 8), "lev": l}

    pending = {}

    def begin(key, start, sent, arrived):
        start()
        pending[key] = [arrived, sent]

    def left(*keys):
        for key in keys:
            pending[key][1]()
            pending[key][1] = lambda: None

    def arrive(*keys):
        for key in keys:
            pending[key][0]()
            pending[key][0] = None

    barrier = pltpu.get_barrier_semaphore()
    greeted = [at(rem(z + dz, 8), rem(x + dx, 4)) for dx in (2, 1, 3, 0) for dz in (2, 6)]
    greeted += [at(rem(z + 1, 8), x), at(rem(z + 7, 8), x), low, high]
    for device in greeted:
        pl.semaphore_signal(barrier, inc=1, device_id=device, device_id_type=MESH)
    x_load = pltpu.make_async_copy(x_ref.at[0], x_vmem, i_sem.at[0])
    w_load = pltpu.make_async_copy(w_ref.at[0], w_vmem, i_sem.at[1])
    c_load = [pltpu.make_async_copy(ref.at[0], c_vmem.at[n], i_sem.at[2 + n]) for n, ref in enumerate((c1_ref, c2_ref))]
    c_load[0].start()
    c_load[1].start()
    x_load.start()
    w_load.start()

    flip_i = f_ref[0, 0]
    flip_j = f_ref[0, 1]
    c_tmp[...] = jnp.zeros((128, 128), jnp.float32)
    for n in range(2):
        c_load[n].wait()
        for i in range(8):
            c_tmp[64 * n + 8 * i:64 * n + 8 * i + 8, 0:LEV] = c_vmem[n, i]
    turned = c_tmp[...].T
    c_send[...] = turned[0:24]
    c_send[18:19, :] = jnp.full((1, 128), flip_i, jnp.int32).astype(jnp.float32)
    c_send[19:20, :] = jnp.full((1, 128), flip_j, jnp.int32).astype(jnp.float32)

    x_load.wait()
    turn = jnp.full((8, 128), flip_j, jnp.int32) == 1

    def pack(n, carry):
        levels = [2 * n, 2 * n + 1]
        for lev in levels:
            for i in range(8):
                fb[SUBSTEPS - 1, lev, pl.ds(i, 8, stride=8), :] = x_vmem[i + flip_i * (7 - 2 * i), lev]
        for lev in levels:
            rows = [fb[SUBSTEPS - 1, lev, 8 * j:8 * j + 8, :] for j in range(8)]
            rows = [jnp.where(turn, rows[7 - j], rows[j]) for j in range(8)]
            for d, v in enumerate(pick_blocks(turn_blocks(rows))):
                send[d, lev] = v
        return carry

    lax.fori_loop(0, LEV // 2, pack, 0)

    pl.semaphore_wait(barrier, len(greeted))

    def block_of(zz, xx):
        return div(rem(zz + 6, 8), 4) * 4 + xx

    def ring_copy(o, sending):
        dz, dx = (2, 6)[o // 4], o % 4
        if sending:
            return rem(z + dz, 8), rem(x + dx, 4), ring
        zs, xs = rem(z + 8 - dz, 8), rem(x + 4 - dx, 4)
        return zs, xs, div(zs, 4) * 4 + xs

    def c_copy(o, sending=True):
        zz, xx, slot = ring_copy(o, sending)
        return pltpu.make_async_remote_copy(
            src_ref=c_send, dst_ref=c_recv.at[pl.ds(slot * 24, 24)],
            send_sem=c_ssem.at[o], recv_sem=c_rsem.at[o], device_id=at(zz, xx), device_id_type=MESH)

    def a_copy(o, ch, sending=True):
        first, count = CHUNKS[ch]
        zz, xx, slot = ring_copy(o, sending)
        return pltpu.make_async_remote_copy(
            src_ref=send.at[block_of(zz, xx), pl.ds(first, count)], dst_ref=recv.at[slot, pl.ds(first, count)],
            send_sem=a_ssem.at[o, ch], recv_sem=a_rsem.at[o, ch], device_id=at(zz, xx), device_id_type=MESH)

    order = [2, 6, 1, 5, 3, 7, 0, 4]
    for o in order:
        begin(("c", o), c_copy(o).start, c_copy(o).wait_send, c_copy(o, False).wait_recv)
    def exchange(ch):
        for o in order:
            begin(("a", ch, o), a_copy(o, ch).start, a_copy(o, ch).wait_send, a_copy(o, ch, False).wait_recv)

    exchange(0)
    w_load.wait()
    diagonal = jnp.where(
        lax.broadcasted_iota(jnp.int32, (72, 72), 0) == lax.broadcasted_iota(jnp.int32, (72, 72), 1), 0.6, 0.0)

    def prepare(cell, carry):
        s, j = cell // 8, cell % 8
        w = w_vmem[s, j]
        total = jnp.sum(w, axis=-1, keepdims=True)
        matrix[cell] = 0.4 * (w / total) + diagonal
        return carry

    lax.fori_loop(0, 16, prepare, 0)

    arrive(*(("c", o) for o in range(8)))
    spread = (
        lax.broadcasted_iota(jnp.int32, (24, 128), 0) % 8 == lax.broadcasted_iota(jnp.int32, (24, 128), 1) // 16
    ).astype(jnp.float32).astype(jnp.bfloat16)

    def spread_level(lev):
        v = c_recv[pl.ds(lev, 8, stride=24), :]
        p0 = v.astype(jnp.bfloat16).astype(jnp.float32)
        p1 = (v - p0).astype(jnp.bfloat16).astype(jnp.float32)
        p2 = v - p0 - p1
        parts = jnp.concatenate([p0, p1, p2], axis=0).astype(jnp.bfloat16)
        return lax.dot_general(parts, spread, (((0,), (0,)), ((), ())), preferred_element_type=jnp.float32)

    def courant(first, width, n, carry):
        levels = [first + width * n + u for u in range(width)]
        for u, lev in enumerate(levels):
            wide = spread_level(lev)
            for i in range(8):
                for n, value in enumerate(coefficients(wide[8 * i:8 * i + 8])):
                    k1[n, lev, 8 * i + 8:8 * i + 16, :] = value
                    if i == 7:
                        k1[n, lev, 0:8, :] = pltpu.roll(value, 16, 1)
                raw[u, pl.ds(i, 8, stride=8), :] = wide[64 + 8 * i:72 + 8 * i]
        for u, lev in enumerate(levels):
            for j in range(8):
                for n, value in enumerate(coefficients(raw[u, 8 * j:8 * j + 8, :])):
                    k2[n, lev, 8 * j + 8:8 * j + 16, :] = value
            edge_send[lev] = raw[u, 56:64, :]
        return carry

    def edge_copy(ch):
        part = pl.ds(*CHUNKS[ch])
        return pltpu.make_async_remote_copy(
            src_ref=edge_send.at[part], dst_ref=edge_recv.at[part],
            send_sem=e_ssem.at[ch], recv_sem=e_rsem.at[ch], device_id=high, device_id_type=MESH)

    def courant_chunk(ch):
        first, count = CHUNKS[ch]
        width = 3 if count % 3 == 0 else 2
        lax.fori_loop(0, count // width, functools.partial(courant, first, width), 0)
        edge = edge_copy(ch)
        begin(("e", ch), edge.start, edge.wait_send, edge.wait_recv)

    roll_low = jnp.where(yc == 0, 16, 0)
    roll_high = jnp.where(yc == 7, 112, 0)
    arrival_turn = [16 * rem(slot + 8 - eighth, 8) for slot in range(8)]
    column_turn = [16 * rem(slot + 8 - ring, 8) for slot in range(8)]

    def unpack(ch):
        first, count = CHUNKS[ch]
        arrive(*(("a", ch, o) for o in range(8)))

        def some(n, carry):
            levels = [first + 2 * n, first + 2 * n + 1]
            for lev in levels:
                rows = pick_blocks([pltpu.roll(recv[slot, lev], arrival_turn[slot], 1) for slot in range(8)])
                for j, v in enumerate(turn_back(rows)):
                    fa[lev, pl.ds(j, 8, stride=8), :] = v
            return carry

        lax.fori_loop(0, count // 2, some, 0)

    def advance(q, low_cells, high_cells, k, lev):
        e = low_cells + q + high_cells
        a = [face_value(*e[n:n + 4]) for n in range(11)]
        flux = [
            face_flux(a[f + 1], a[f], a[f + 2], e[f + 2], e[f + 3], *(k[n, lev, 8 * f:8 * f + 8, :] for n in range(3)))
            for f in range(9)]
        return [q[n] - (flux[n + 1] - flux[n]) for n in range(8)]

    def sweep_first(step, ch):
        first, count = CHUNKS[ch]

        def level(lev):
            q = [fa[lev, 8 * i:8 * i + 8, :] for i in range(8)]
            return advance(q, [pltpu.roll(v, 16, 1) for v in q[5:]], [pltpu.roll(v, 112, 1) for v in q[:3]], k1, lev)

        def some(n, carry):
            levels = [first + n * UNROLL + k for k in range(UNROLL)]
            new = [level(lev) for lev in levels]
            for lev, rows in zip(levels, new):
                for i in range(8):
                    fb[step, lev, pl.ds(i, 8, stride=8), :] = rows[i]
            return carry

        lax.fori_loop(0, count // UNROLL, some, 0)

    def halo_copies(step, ch):
        first, count = CHUNKS[ch]
        return (
            pltpu.make_async_remote_copy(
                src_ref=fb.at[step, pl.ds(first, count), pl.ds(40, 24)], dst_ref=halo_low.at[step, pl.ds(first, count)],
                send_sem=h_ssem.at[0, step, ch], recv_sem=h_rsem.at[0, step, ch], device_id=high, device_id_type=MESH),
            pltpu.make_async_remote_copy(
                src_ref=fb.at[step, pl.ds(first, count), pl.ds(0, 24)], dst_ref=halo_high.at[step, pl.ds(first, count)],
                send_sem=h_ssem.at[1, step, ch], recv_sem=h_rsem.at[1, step, ch], device_id=low, device_id_type=MESH),
        )

    def sweep_second(step, ch):
        first, count = CHUNKS[ch]
        last = step == SUBSTEPS - 1

        def level(lev):
            q = [fb[step, lev, 8 * j:8 * j + 8, :] for j in range(8)]
            new = advance(
                q, [pltpu.roll(halo_low[step, lev, 8 * j:8 * j + 8, :], roll_low, 1) for j in range(3)],
                [pltpu.roll(halo_high[step, lev, 8 * j:8 * j + 8, :], roll_high, 1) for j in range(3)], k2, lev)
            if last:
                back = flags[1] > 0.5
                new = [jnp.where(back, new[7 - j], new[j]) for j in range(8)]
            return new

        def some(n, carry):
            levels = [first + n * UNROLL + k for k in range(UNROLL)]
            new = [level(lev) for lev in levels]
            for lev, rows in zip(levels, new):
                for j in range(8):
                    fa[lev, pl.ds(j, 8, stride=8), :] = rows[j]
            return carry

        lax.fori_loop(0, count // UNROLL, some, 0)

    def edge_chunk(ch):
        first, count = CHUNKS[ch]
        arrive(("e", ch))

        def some(n, carry):
            for lev in [first + 2 * n, first + 2 * n + 1]:
                for n, value in enumerate(coefficients(pltpu.roll(edge_recv[lev], roll_low, 1))):
                    k2[n, lev, 0:8, :] = value
            return carry

        lax.fori_loop(0, count // 2, some, 0)

    def mix_pack(ch):
        groups = GROUPS[ch]

        def one(r, carry):
            back = flags[0] > 0.5
            for m in groups:
                rows = []
                for k in range(8):
                    lev, i = 4 * m + k // 2, 2 * r + k % 2
                    if lev < LEV:
                        here = fa[lev, pl.ds(pl.multiple_of(8 * i, 8), 8), :]
                        there = fa[lev, pl.ds(pl.multiple_of(56 - 8 * i, 8), 8), :]
                        rows.append(jnp.where(back, there, here))
                    else:
                        rows.append(jnp.zeros((8, 128), jnp.float32))
                for k, v in enumerate(pick_blocks(turn_blocks(rows))):
                    mix_send[k * 4 + r, m] = v
            return carry

        lax.fori_loop(0, 4, one, 0)

    def m_copy(o, ch):
        dz, dx = (o // 4, o % 4) if isinstance(o, int) else (div(o, 4), rem(o, 4))
        zd, xd = rem(z + dz, 8), rem(x + dx, 4)
        part = pl.ds(GROUPS[ch][0], len(GROUPS[ch]))
        return pltpu.make_async_remote_copy(
            src_ref=mix_send.at[(div(zd, 4) * 4 + xd) * 4 + rem(zd, 4), part], dst_ref=mix_recv.at[group * 8 + eighth, part],
            send_sem=m_ssem.at[ch, o], recv_sem=m_rsem.at[ch, o], device_id=at(zd, xd), device_id_type=MESH)

    def m_arrival(o, ch):
        zs, xs = rem(z + 8 - div(o, 4), 8), rem(x + 4 - rem(o, 4), 4)
        slot = rem(zs + 2, 4) * 8 + block_of(zs, xs)
        part = pl.ds(GROUPS[ch][0], len(GROUPS[ch]))
        return pltpu.make_async_remote_copy(
            src_ref=mix_send.at[0, part], dst_ref=mix_recv.at[slot, part],
            send_sem=m_ssem.at[ch, o], recv_sem=m_rsem.at[ch, o], device_id=at(zs, xs), device_id_type=MESH)

    own = [
        pltpu.make_async_copy(
            mix_send.at[ring * 4 + l, pl.ds(groups[0], len(groups))],
            mix_recv.at[group * 8 + eighth, pl.ds(groups[0], len(groups))], l_sem.at[2 + ch])
        for ch, groups in enumerate(GROUPS)
    ]

    def segment(step, ch):
        if step == 0:
            unpack(ch)
        else:
            if step == 1:
                edge_chunk(ch)
            arrive(("h", step - 1, ch, 0), ("h", step - 1, ch, 1))
            sweep_second(step - 1, ch)
        if step < SUBSTEPS:
            sweep_first(step, ch)
            for side, copy in enumerate(halo_copies(step, ch)):
                begin(("h", step, ch, side), copy.start, copy.wait_send, copy.wait_recv)

    def others(action):
        def run():
            def one(o, carry):
                action(o)
                return carry

            lax.fori_loop(1, 32, one, 0)

        return run

    def scatter(ch):
        mix_pack(ch)

        def far_first():
            hops = lambda o: min(o // 4, 8 - o // 4) + min(o % 4, 4 - o % 4)
            for o in sorted(range(1, 32), key=hops, reverse=True):
                m_copy(o, ch).start()

        begin(
            ("m", ch), far_first,
            others(lambda o: m_copy(o, ch).wait_send()), others(lambda o: m_arrival(o, ch).wait_recv()))
        begin(("own", ch), own[ch].start, lambda: None, own[ch].wait)

    for what, ch, *step in SCHEDULE:
        if what == "send":
            left(*(("a", ch - 1, o) for o in range(8)))
            exchange(ch)
        elif what == "flags":
            for n in range(2):
                flags[n] = spread_level(LEV + n)[0:8]
        elif what == "courant":
            courant_chunk(ch)
        elif what == "scatter":
            scatter(ch)
        else:
            segment(step[0], ch)

    def mix_unpack(ch):
        def one(g, carry):
            for m in GROUPS[ch]:
                rows = pick_blocks([pltpu.roll(mix_recv[g * 8 + k, m], column_turn[k], 1) for k in range(8)])
                rows = turn_back(rows)
                for k in range(8):
                    lev, s = 4 * m + k // 2, k % 2
                    if lev < LEV:
                        columns[s, pl.ds(pl.multiple_of((g * LEV + lev) * 8, 8), 8), :] = rows[k]
            return carry

        lax.fori_loop(0, 4, one, 0)

    for ch in range(NCH):
        arrive(("m", ch), ("own", ch))
        mix_unpack(ch)

    def d_copy(s, o):
        to = rem(l + o, 4)
        return pltpu.make_async_remote_copy(
            src_ref=mixed.at[s, pl.ds(to * 144, 144)], dst_ref=o_ref.at[0, 2 * l + s],
            send_sem=d_ssem.at[s, o], recv_sem=d_rsem.at[s, o], device_id={"tile": t, "lev": to}, device_id_type=MESH)

    def d_arrival(s, o):
        source = rem(l + 4 - o, 4)
        return pltpu.make_async_remote_copy(
            src_ref=mixed.at[s, pl.ds(0, 144)], dst_ref=o_ref.at[0, 2 * source + s],
            send_sem=d_ssem.at[s, o], recv_sem=d_rsem.at[s, o], device_id={"tile": t, "lev": source}, device_id_type=MESH)

    def mix_row(s):
        def cell(j):
            v = columns[s, pl.ds(j, 72, stride=8), :]
            v_hi = v.astype(jnp.bfloat16)
            v_lo = (v - v_hi.astype(jnp.float32)).astype(jnp.bfloat16)
            m = matrix[s * 8 + j]
            m_hi = m.astype(jnp.bfloat16)
            m_lo = (m - m_hi.astype(jnp.float32)).astype(jnp.bfloat16)
            dot = lambda a, b: jnp.dot(a, b, preferred_element_type=jnp.float32)
            out = dot(m_hi, v_hi) + (dot(m_hi, v_lo) + dot(m_lo, v_hi))
            mixed[s, pl.ds(j, 72, stride=8), :] = out

        def some(n, carry):
            for j in range(CELLS):
                cell(CELLS * n + j)
            return carry

        lax.fori_loop(0, 8 // CELLS, some, 0)

    for s in range(2):
        mix_row(s)
        for o in (2, 3, 1):
            begin(("d", s, o), d_copy(s, o).start, d_copy(s, o).wait_send, d_arrival(s, o).wait_recv)
        local = pltpu.make_async_copy(mixed.at[s, pl.ds(l * 144, 144)], o_ref.at[0, 2 * l + s], l_sem.at[s])
        begin(("local", s), local.start, lambda: None, local.wait)

    for arrived, sent in pending.values():
        if arrived is not None:
            arrived()
        sent()


def hand_over(i_ref, o_ref, v_ref, i_sem, o_sem):
    parts = [pl.ds(2 * n, 2) for n in range(4)]
    fetch = [pltpu.make_async_copy(i_ref.at[0, p], v_ref.at[p], i_sem.at[n]) for n, p in enumerate(parts)]
    store = [pltpu.make_async_copy(v_ref.at[p], o_ref.at[0, p], o_sem.at[n]) for n, p in enumerate(parts)]
    for copy in fetch:
        copy.start()
    for one, two in zip(fetch, store):
        one.wait()
        two.start()
    for copy in store:
        copy.wait()


def solution(mesh):
    f32 = jnp.float32

    def on_device(tracers, courant_first, courant_second, weights, frame_flip):
        hbm = pl.BlockSpec(memory_space=pl.ANY)
        dma = pltpu.SemaphoreType.DMA
        rows = jnp.transpose(tracers, (0, 1, 3, 2, 4)).reshape(1, 8, LEV, 8, 128)
        out = pl.pallas_call(
            kernel,
            out_shape=jax.ShapeDtypeStruct((1, 8, LEV * 8, 128), f32),
            in_specs=[hbm, hbm, hbm, hbm, pl.BlockSpec(memory_space=pltpu.SMEM)],
            out_specs=hbm,
            scratch_shapes=[
                pltpu.VMEM((8, LEV, 8, 128), f32),
                pltpu.VMEM((2, 8, 8, LEV), f32),
                pltpu.VMEM((2, 8, 72, 72), f32),
                pltpu.VMEM((8, LEV, 8, 128), f32),
                pltpu.VMEM((8, LEV, 8, 128), f32),
                pltpu.VMEM((128, 128), f32),
                pltpu.VMEM((24, 128), f32),
                pltpu.VMEM((192, 128), f32),
                pltpu.VMEM((3, 64, 128), f32),
                pltpu.VMEM((2, 8, 128), f32),
                pltpu.VMEM((LEV, 64, 128), f32),
                pltpu.VMEM((SUBSTEPS, LEV, 64, 128), f32),
                pltpu.VMEM((SUBSTEPS, LEV, 24, 128), f32),
                pltpu.VMEM((SUBSTEPS, LEV, 24, 128), f32),
                pltpu.VMEM((LEV, 8, 128), f32),
                pltpu.VMEM((LEV, 8, 128), f32),
                pltpu.VMEM((3, LEV, 72, 128), f32),
                pltpu.VMEM((3, LEV, 72, 128), f32),
                pltpu.VMEM((32, 5, 8, 128), f32),
                pltpu.VMEM((32, 5, 8, 128), f32),
                pltpu.VMEM((2, 72 * 8, 128), f32),
                pltpu.VMEM((16, 72, 72), f32),
                pltpu.VMEM((2, 72 * 8, 128), f32),
                dma((8, NCH)), dma((8, NCH)),
                dma((8,)), dma((8,)),
                dma((2, SUBSTEPS, NCH)), dma((2, SUBSTEPS, NCH)),
                dma((NCH,)), dma((NCH,)),
                dma((NCH, 32)), dma((NCH, 32)),
                dma((2, 4)), dma((2, 4)),
                dma((2 + NCH,)),
                dma((4,)),
            ],
            compiler_params=pltpu.CompilerParams(collective_id=0, has_side_effects=True),
        )(rows, courant_first, courant_second, weights, frame_flip)
        out = pl.pallas_call(
            hand_over,
            out_shape=jax.ShapeDtypeStruct((1, 8, LEV * 8, 128), f32),
            in_specs=[hbm],
            out_specs=hbm,
            scratch_shapes=[pltpu.VMEM((8, LEV * 8, 128), f32), dma((4,)), dma((4,))],
        )(out)
        return jnp.transpose(out.reshape(1, 8, LEV, 8, 128), (0, 1, 3, 2, 4))

    return jax.shard_map(
        on_device,
        mesh=mesh,
        in_specs=(
            P("tile", None, None, "lev", None),
            P("tile", None, None, "lev"),
            P("tile", None, None, "lev"),
            P("tile", "lev", None, None, None),
            P("tile", None),
        ),
        out_specs=P("tile", None, None, "lev", None),
        check_vma=False,
    )
```
